32 devices in a mesh: shot: 4 (over z), slab: 8 (over y, x, core).
Axes of the slice: x: 2, y: 2, z: 4, core: 2. Of those that a mesh axis runs over, the one named last changes fastest.
Arguments:
- source_field: bfloat16 [4, 256, 384, 512], P('shot', 'slab'), may hold values from -6 to 6
- receiver_fields: bfloat16 [8, 256, 384, 512], P('shot', 'slab'), may hold values from -6 to 6
- weights: int32 [8], P('shot'), may hold values from -1 to 1, as said below
- model: bfloat16 [256, 384, 512], P(('slab', 'shot')), may hold values from -6 to 6
- wedge_sizes: int32 [16], replicated, may hold values from 1 to 95, as said below
- wedge_scales: float32 [16], replicated, may hold values from 0.3 to 3
Outputs:
- new_model: float32 [256, 384, 512], P(('slab', 'shot'))
The draws below stay inside these ranges and needn't reach their ends.
Inputs may be any that keep to these rules, and one draw needn't show every extreme that they name: `weights`: each weight is -1 or +1. `wedge_sizes`: wedges 2d and 2d + 1 together hold either 512 // 8 // 2 or 96 columns, each count for half of the pairs; every wedge holds one column or more; all sizes sum to 512.
All inputs are finite; a program needn't handle non-finite values.
Results may differ from the reference program's by a relative error of at most 0.0003.
Values sent between devices are 32-bit elements; how exact they have to be, the bound alone decides.
A program may use at most 128 MiB of HBM per device.

```python
import math
import jax
import jax.numpy as jnp
from jax import lax

NZ = 256
NY = 384
NX = 512
SH_DEV = 2
GROUPS = 4
SHOTS = 8
NWEDGE = 16
N_SHOT = 4
N_SLAB = 8


def draw_weights(key, part):
    return 2 * jax.random.randint(key, (SH_DEV * N_SHOT,), 0, 2, dtype=jnp.int32) - 1


def draw_wedge_sizes(key, part):
    first_key = jax.random.fold_in(key, 11)
    second_key = jax.random.fold_in(key, 23)
    share = NX // N_SLAB
    half = N_SLAB // 2
    pattern = jnp.concatenate([jnp.full((half,), share // 2, jnp.int32), jnp.full((N_SLAB - half,), 3 * share // 2, jnp.int32)])
    totals = pattern[jax.random.permutation(first_key, N_SLAB)]
    raw = jax.random.randint(second_key, (N_SLAB,), 0, 1 << 20, dtype=jnp.int32)
    leading = 1 + raw % jnp.maximum(totals - 1, 1)
    trailing = totals - leading
    return jnp.stack([leading, trailing], axis=1).reshape(-1).astype(jnp.int32)


def level_of(own_key, shape, shards, low, top_value):
    factor_of = 1.0
    for dim, shards_of in shards:
        draws = jax.random.uniform(jax.random.fold_in(jax.random.fold_in(own_key, 6), dim), (shards_of,), jnp.float32, low / len(shards), top_value / len(shards))
        factor_of = factor_of * jnp.repeat(jnp.exp(draws), shape[dim] // shards_of).reshape((-1,) + (1,) * (len(shape) - 1 - dim))
    return factor_of


def noise(stream_key, dims, width, bound, split=(), kind=jnp.bfloat16):
    gain = level_of(stream_key, dims, split, -0.22, 0.18) if split else 1.0
    drawn = jax.random.normal(stream_key, dims, jnp.float32) * width * gain
    return jnp.minimum(jnp.maximum(drawn, -bound), bound).astype(kind)


def setup_inputs(seed: int = 0) -> dict:
    keys = jax.random.split(jax.random.key(seed), 7)
    return {
        "source_field": noise(keys[0], (GROUPS, NZ, NY, NX), 1.0, 6.0, ((0, 4), (1, 8))),
        "receiver_fields": noise(keys[1], (SHOTS, NZ, NY, NX), 1.0, 6.0, ((0, 4), (1, 8))),
        "weights": draw_weights(jax.random.fold_in(keys[6], 71), 0),
        "model": noise(keys[3], (NZ, NY, NX), 1.0, 6.0, ((0, 32),)),
        "wedge_sizes": draw_wedge_sizes(jax.random.fold_in(keys[6], 71), 0),
        "wedge_scales": jnp.clip(jnp.exp(jax.random.uniform(keys[5], (NWEDGE,), jnp.float32, math.log(0.3), math.log(3.0))), 0.3, 3.0),
    }


STEP_SIZE = 0.25
EPSILON = 1e-06

def reference(source_field, receiver_fields, weights, model, wedge_sizes, wedge_scales):
    groups = source_field.shape[0]
    per_group = receiver_fields.shape[0] // groups
    signs = weights.astype(jnp.float32).reshape(groups, per_group)
    receivers = receiver_fields.reshape((groups, per_group) + receiver_fields.shape[1:])

    def add_group(total, inputs):
        source, group_fields, group_signs = inputs
        encoded = jnp.zeros(source.shape, jnp.float32)
        for member in range(per_group):
            encoded = encoded + group_signs[member] * group_fields[member].astype(jnp.float32)
        return (total + source.astype(jnp.float32) * encoded, None)
    gradient, _ = lax.scan(add_group, jnp.zeros(model.shape, jnp.float32), (source_field, receivers, signs))
    update = model.astype(jnp.float32) - STEP_SIZE * gradient
    spectrum = jnp.fft.fftn(update)
    depth, rows, columns = update.shape
    ends = jnp.cumsum(wedge_sizes).astype(jnp.int32)
    starts = (ends - wedge_sizes).astype(jnp.int32)
    column = jnp.arange(columns, dtype=jnp.int32)
    member_of = ((column[:, None] >= starts[None, :]) & (column[:, None] < ends[None, :])).astype(jnp.float32)
    energy = jnp.real(spectrum) ** 2 + jnp.imag(spectrum) ** 2
    column_power = lax.optimization_barrier(jnp.sum(energy, axis=(0, 1)))
    wedge_power = jnp.dot(column_power, member_of, precision=lax.Precision.HIGHEST)
    entries = wedge_sizes.astype(jnp.float32) * (depth * rows)
    spread = jnp.sqrt(wedge_power / entries + EPSILON)
    level = jnp.dot(member_of, wedge_scales * spread, precision=lax.Precision.HIGHEST)
    magnitude = jnp.sqrt(energy)
    factor = jnp.maximum(magnitude - level, 0.0) / jnp.maximum(magnitude, level)
    return jnp.real(jnp.fft.ifftn(spectrum * factor)).astype(jnp.float32)
```

```python
import functools

import jax
import jax.numpy as jnp
import numpy as np
from jax import lax
from jax.experimental import pallas as pl
from jax.experimental.pallas import tpu as pltpu
from jax.sharding import PartitionSpec as P

STEP_SIZE = 0.25
EPSILON = 1e-06
HIGHEST = lax.Precision.HIGHEST
LANES = 128
LAG = 2
F32 = jnp.float32
BF16 = jnp.bfloat16
MESH = pl.DeviceIdType.MESH
VMEM_LIMIT = 60 * 1024 * 1024


def halves(x):
    high = x.astype(BF16)
    return high, (x - high.astype(F32)).astype(BF16)


def host_halves(table):
    table = table.astype(np.float32)
    high = table.astype(BF16)
    low = (table - high.astype(np.float32)).astype(BF16)
    return np.stack([high, low])


def dot3(a, b, dims=((1,), (0,))):
    product = functools.partial(
        lax.dot_general, dimension_numbers=(dims, ((), ())), preferred_element_type=F32
    )
    return product(a[0], b[0]) + (product(a[0], b[1]) + product(a[1], b[0]))


def circle(rows, columns, length):
    angle = (np.outer(rows, columns) % length) * (2.0 * np.pi / length)
    return np.cos(angle), np.sin(angle)


def x_table(parity, width):
    half = width // 2
    cosine, sine = circle(2 * np.arange(half // 2) + parity, np.arange(half), width)
    sine = -sine
    if parity == 0:
        sine[0] = 1.0 - 2.0 * (np.arange(half) % 2)
    return np.stack([cosine, sine], axis=1)


def reduce_forward(
    shots, slabs, sign_ref, source_ref, recv_ref, model_ref, tx_ref, g_ref, power_ref,
    acc, along_x, source_buf, recv_buf, model_buf, in_sem, chain_send, chain_recv, ex_send, ex_recv, own_sem,
):
    shot = lax.axis_index("shot")
    slab = lax.axis_index("slab")
    local, height, width = source_ref.shape
    planes = model_ref.shape[0]
    half = width // 2
    pieces = height // LANES
    chunks = local * pieces
    groups = g_ref.shape[0]
    rows = along_x.shape[4]
    hops = (shots - 1 - shot, shot)
    last = shots - 1
    base = chunks * (1 + 4 * LAG * shots // chunks)

    def inputs(way, chunk):
        slot = lax.rem(chunk, 2)
        plane = chunk // pieces
        span = pl.ds(pl.multiple_of(lax.rem(chunk, pieces) * LANES, LANES), LANES)
        return (
            pltpu.make_async_copy(
                source_ref.at[plane, span], source_buf.at[way, slot], in_sem.at[way, slot, 0]
            ),
            pltpu.make_async_copy(
                recv_ref.at[:, plane, span], recv_buf.at[way, slot], in_sem.at[way, slot, 1]
            ),
        )

    def own_model(way, chunk):
        slot = lax.rem(chunk, 2)
        plane = chunk // pieces
        span = pl.ds(pl.multiple_of(lax.rem(chunk, pieces) * LANES, LANES), LANES)
        return pltpu.make_async_copy(
            model_ref.at[lax.rem(plane, planes), span], model_buf.at[way, slot], in_sem.at[way, slot, 2]
        )

    def owned(chunk):
        return chunk // pieces // planes == shot

    def exchange(plane, other):
        return pltpu.make_async_remote_copy(
            src_ref=along_x.at[plane, other],
            dst_ref=g_ref.at[:, :, pl.ds(pl.multiple_of((slab * local + plane) * rows, rows), rows)],
            send_sem=ex_send.at[other],
            recv_sem=ex_recv.at[slab],
            device_id=(shot, other),
            device_id_type=MESH,
        )

    def keep(plane):
        return pltpu.make_async_copy(
            along_x.at[plane, slab],
            g_ref.at[:, :, pl.ds(pl.multiple_of((slab * local + plane) * rows, rows), rows)],
            own_sem,
        )

    def join(way, low, high):
        return low + high if way == 0 else low - high

    power_ref[...] = jnp.zeros_like(power_ref)

    def step(t, carry):
        for way in range(2):
            count = t + base - LAG * hops[way]
            chunk = lax.rem(count, chunks)

            @pl.when((count >= base) & (count < base + chunks))
            def _():
                for copy in inputs(way, chunk):
                    copy.start()

                @pl.when(owned(chunk))
                def _():
                    own_model(way, chunk).start()

        for way in range(2):
            count = t - 1 + base - LAG * hops[way]
            chunk = lax.rem(count, chunks)

            @pl.when((count >= base) & (count < base + chunks))
            def _():
                slot = lax.rem(chunk, 2)
                for copy in inputs(way, chunk):
                    copy.wait()
                encoded = jnp.zeros((LANES, width), F32)
                for member in range(recv_ref.shape[0]):
                    encoded = encoded + sign_ref[member].astype(F32) * recv_buf[way, slot, member].astype(F32)
                part = -STEP_SIZE * (source_buf[way, slot].astype(F32) * encoded)
                part = join(way, part[:, :half], part[:, half:])

                @pl.when(hops[way] > 0)
                def _():
                    arrived = acc.at[way, chunk]
                    pltpu.make_async_copy(arrived, arrived, chain_recv.at[way, chunk]).wait()
                    acc[way, chunk] = acc[way, chunk] + part

                @pl.when(hops[way] == 0)
                def _():
                    acc[way, chunk] = part

                @pl.when(owned(chunk))
                def _():
                    own_model(way, chunk).wait()
                    image = model_buf[way, slot].astype(F32)
                    acc[way, chunk] = acc[way, chunk] + join(way, image[:, :half], image[:, half:])

                @pl.when(hops[way] < last)
                def _():
                    pltpu.make_async_remote_copy(
                        src_ref=acc.at[way, chunk],
                        dst_ref=acc.at[way, chunk],
                        send_sem=chain_send.at[way],
                        recv_sem=chain_recv.at[way, chunk],
                        device_id=(shot - 1 + 2 * way, slab),
                        device_id_type=MESH,
                    ).start()

                @pl.when(hops[way] == last)
                def _():
                    plane = chunk // pieces
                    piece = lax.rem(chunk, pieces)
                    result = dot3((tx_ref[way, 0], tx_ref[way, 1]), halves(acc[way, chunk]), ((1,), (1,)))
                    power_ref[...] = power_ref[...] + result * result
                    along_x[plane, :, :, piece] = result.reshape(slabs, groups, rows, LANES)

                    @pl.when(piece == pieces - 1)
                    def _():
                        def send(offset, carry):
                            exchange(plane, lax.rem(slab + offset, slabs)).start()
                            return carry

                        lax.fori_loop(1, slabs, send, 0)
                        keep(plane).start()

        return carry

    lax.fori_loop(0, chunks + LAG * last + 1, step, 0)

    for way in range(2):

        @pl.when(hops[way] < last)
        def _():
            sent = acc.at[way]
            pltpu.make_async_copy(sent, sent, chain_send.at[way]).wait()

    @pl.when((shot == 0) | (shot == last))
    def _():
        def part_of(other):
            return g_ref.at[:, :, pl.ds(pl.multiple_of(other * local * rows, rows), local * rows)]

        def finish(offset, carry):
            other = lax.rem(slab + offset, slabs)
            piece = part_of(other)
            pltpu.make_async_copy(piece, piece, ex_send.at[other]).wait()
            pltpu.make_async_copy(piece, piece, ex_recv.at[other]).wait()
            return carry

        lax.fori_loop(1, slabs, finish, 0)
        mine = part_of(slab)
        pltpu.make_async_copy(mine, mine, own_sem).wait()


def shrink_back(
    shots, slabs, level_ref, scale_ref, tz_ref, ty_ref, g_ref, r_ref, held, out, send_sem, recv_sem, own_sem
):
    slot = pl.program_id(0)
    shot = lax.axis_index("shot")
    slab = lax.axis_index("slab")
    slots, _, pieces, depth, _ = out.shape
    width = pieces * LANES
    planes = r_ref.shape[4]
    rows = g_ref.shape[1] // depth
    devices = shots * slabs
    last = shots - 1
    end = (shot == 0) | (shot == last)
    me = jnp.where(shot == 0, 0, slabs) + slab

    def along_y(re, im, sign):
        result = dot3(halves(jnp.concatenate([re, im], axis=0)), (ty_ref[0], ty_ref[1]))
        with_cos, with_sin = result[:, :width], result[:, width:]
        return (
            with_cos[:depth] + sign * with_sin[depth:],
            with_cos[depth:] - sign * with_sin[:depth],
        )

    def along_z(re, im, sign):
        result = dot3((tz_ref[0], tz_ref[1]), halves(jnp.concatenate([re, im], axis=1)))
        with_cos, with_sin = result[:depth], result[depth:]
        return (
            with_cos[:, :width] + sign * with_sin[:, width:],
            with_cos[:, width:] - sign * with_sin[:, :width],
        )

    def target(index):
        far = index // slabs
        to_shot = jnp.where(shot == 0, last - far, far)
        to_slab = lax.rem(slab + index, slabs)
        return to_shot, to_slab

    def part(to_shot, to_slab):
        first = to_slab * (shots * planes) + to_shot * planes
        return out.at[slot, :, :, pl.ds(pl.multiple_of(first, planes), planes)]

    @pl.when(end)
    def _():
        packed = (shot == 0) & (slab == 0) & (slot == 0)
        row = lax.rem(slot, rows // 2)

        def spread(first):
            return jnp.concatenate(
                [g_ref[piece, pl.ds(first, depth, stride=rows), :] for piece in range(pieces)], axis=1
            )

        def column(which, carry):
            re = spread(row + which * (rows // 2))
            im = jnp.where(packed, 0.0, spread(row + rows // 2))
            re, im = along_z(*along_y(re, im, 1.0), 1.0)
            index = slot + which * slots
            magnitude = jnp.sqrt(re * re + im * im)
            total = 0.0
            for side in range(2):
                level = level_ref[side, index]
                total = total + jnp.maximum(magnitude - level, 0.0) / jnp.maximum(magnitude, level)
            total = total * scale_ref[index]
            re, im = re * total, im * total

            @pl.when(which == 0)
            def _():
                held[0] = re
                held[1] = im

            @pl.when(which == 1)
            def _():
                held[0] = held[0] - im
                held[1] = held[1] + re

            return carry

        lax.fori_loop(0, jnp.where(packed, 2, 1), column, 0)
        re, im = along_y(*along_z(held[0], held[1], -1.0), -1.0)
        for piece in range(pieces):
            span = slice(piece * LANES, (piece + 1) * LANES)
            out[slot, 0, piece] = re[:, span]
            out[slot, 1, piece] = im[:, span]

        def send(index, carry):
            to_shot, to_slab = target(index)

            @pl.when((to_shot != shot) | (to_slab != slab))
            def _():
                pltpu.make_async_remote_copy(
                    src_ref=part(to_shot, to_slab),
                    dst_ref=r_ref.at[me, slot],
                    send_sem=send_sem.at[to_shot, to_slab],
                    recv_sem=recv_sem.at[me],
                    device_id=(to_shot, to_slab),
                    device_id_type=MESH,
                ).start()

            return carry

        lax.fori_loop(0, devices, send, 0)
        pltpu.make_async_copy(part(shot, slab), r_ref.at[me, slot], own_sem).start()

    @pl.when(slot == slots - 1)
    def _():
        @pl.when(end)
        def _():
            def sent(index, carry):
                to_shot, to_slab = target(index)

                @pl.when((to_shot != shot) | (to_slab != slab))
                def _():
                    pltpu.make_async_copy(r_ref.at[0], r_ref.at[0], send_sem.at[to_shot, to_slab]).wait()

                return carry

            lax.fori_loop(0, devices, sent, 0)
            pltpu.make_async_copy(r_ref.at[me], r_ref.at[me], own_sem).wait()

        def arrived(index, carry):
            @pl.when(jnp.logical_not(end) | (index != me))
            def _():
                pltpu.make_async_copy(r_ref.at[index], r_ref.at[index], recv_sem.at[index]).wait()

            return carry

        lax.fori_loop(0, 2 * slabs, arrived, 0)


def inverse_x(planes, pieces, r_ref, tx_ref, out_ref):
    plane = pl.program_id(0)
    count = tx_ref.shape[2]

    def side(parity):
        pitch = pieces * planes
        terms = jnp.concatenate(
            [
                r_ref[pl.ds(parity * count * pitch + piece * planes + plane, count, stride=pitch), :]
                for piece in range(pieces)
            ],
            axis=1,
        )
        return dot3(halves(terms), (tx_ref[parity, 0], tx_ref[parity, 1]), ((0,), (0,)))

    even, odd = side(0), side(1)
    half = even.shape[1]
    out_ref[0, :, :half] = even + odd
    out_ref[0, :, half:] = even - odd


def whole_block(array, memory_space=None):
    if memory_space is not None:
        return pl.BlockSpec(memory_space=memory_space)
    zeros = (0,) * array.ndim
    return pl.BlockSpec(array.shape, lambda *_: zeros)


def on_device(source_field, receiver_fields, weights, model, wedge_sizes, wedge_scales):
    shots = lax.axis_size("shot")
    slabs = lax.axis_size("slab")
    shot = lax.axis_index("shot")
    slab = lax.axis_index("slab")
    devices = shots * slabs
    members, local, height, width = receiver_fields.shape
    planes = model.shape[0]
    depth = local * slabs
    half = width // 2
    slots = half // 2 // slabs
    four = min(4, slots)
    groups, rows = slots // four, 2 * four
    pieces = height // LANES
    chunks = local * pieces
    params = functools.partial(pltpu.CompilerParams, vmem_limit_bytes=VMEM_LIMIT)

    tables = [x_table(parity, width).reshape(slabs, groups, four, 2, half) for parity in range(2)]
    tx = np.stack([host_halves(t.transpose(0, 1, 3, 2, 4).reshape(half, half)) for t in tables])
    tx_back = np.stack([host_halves(t.reshape(half, half)) for t in tables])
    ty = host_halves(np.concatenate(circle(np.arange(height), np.arange(height), height), axis=1))
    tz = host_halves(np.concatenate(circle(np.arange(depth), np.arange(depth), depth), axis=0))
    tx, tx_back, ty, tz = (jnp.asarray(table) for table in (tx, tx_back, ty, tz))

    anywhere = pl.BlockSpec(memory_space=pl.ANY)
    gathered, power = pl.pallas_call(
        functools.partial(reduce_forward, shots, slabs),
        out_shape=(
            jax.ShapeDtypeStruct((groups, pieces, depth * rows, LANES), F32),
            jax.ShapeDtypeStruct((half, LANES), F32),
        ),
        in_specs=[
            pl.BlockSpec(memory_space=pltpu.SMEM),
            anywhere,
            anywhere,
            anywhere,
            pl.BlockSpec(memory_space=pltpu.VMEM),
        ],
        out_specs=(anywhere, pl.BlockSpec(memory_space=pltpu.VMEM)),
        scratch_shapes=[
            pltpu.VMEM((2, chunks, LANES, half), F32),
            pltpu.VMEM((local, slabs, groups, pieces, rows, LANES), F32),
            pltpu.VMEM((2, 2, LANES, width), BF16),
            pltpu.VMEM((2, 2, members, LANES, width), BF16),
            pltpu.VMEM((2, 2, LANES, width), BF16),
            pltpu.SemaphoreType.DMA((2, 2, 3)),
            pltpu.SemaphoreType.DMA((2,)),
            pltpu.SemaphoreType.DMA((2, chunks)),
            pltpu.SemaphoreType.DMA((slabs,)),
            pltpu.SemaphoreType.DMA((slabs,)),
            pltpu.SemaphoreType.DMA,
        ],
        compiler_params=params(has_side_effects=True),
    )(weights, source_field[0], receiver_fields, model, tx)

    wedges = wedge_sizes.shape[0]
    before = np.tril(np.ones((wedges, wedges), np.int32), -1)
    starts = jnp.sum(before * wedge_sizes[None, :], axis=1)
    ends = starts + wedge_sizes

    def members_of(columns):
        return (
            (columns[:, None] >= starts[None, :]) & (columns[:, None] < ends[None, :])
        ).astype(F32)

    parity = (shot != 0).astype(jnp.int32)
    end = (shot == 0) | (shot == shots - 1)
    row_slots = (
        np.arange(slabs)[:, None, None, None] * slots
        + np.arange(groups)[:, None, None] * four
        + np.zeros((2, 1), np.int64)
        + np.arange(four)
    )
    nyquist = np.zeros((slabs, groups, 2, four), bool)
    nyquist[0, 0, 1, 0] = True
    row_columns = 2 * jnp.asarray(row_slots.reshape(-1), jnp.int32) + parity
    row_columns = jnp.where(jnp.asarray(nyquist.reshape(-1)) & (parity == 0), half, row_columns)
    row_paired = (width - row_columns) % width
    counted = members_of(row_columns) + jnp.where(row_paired == row_columns, 0.0, 1.0)[:, None] * members_of(row_paired)
    own_power = jnp.sum(jnp.sum(power, axis=1)[:, None] * counted, axis=0)
    own_power = jnp.where(end, own_power, 0.0)
    everywhere = jnp.broadcast_to(own_power[None, :], (devices, wedges))
    wedge_power = jnp.sum(
        lax.all_to_all(everywhere, ("shot", "slab"), split_axis=0, concat_axis=0, tiled=True), axis=0
    )
    heights = wedge_scales * jnp.sqrt(wedge_power / wedge_sizes.astype(F32) + EPSILON)

    columns = 2 * (slab * slots + lax.iota(jnp.int32, slots)) + parity
    columns = jnp.concatenate([columns, jnp.full((1,), half, jnp.int32)])
    paired = (width - columns) % width
    levels = jnp.stack(
        [
            jnp.sum(members_of(columns) * heights[None, :], axis=1),
            jnp.sum(members_of(paired) * heights[None, :], axis=1),
        ]
    )
    scale = jnp.where(paired == columns, 0.5, 1.0) * (1.0 / (depth * height * width))

    returned = pl.pallas_call(
        functools.partial(shrink_back, shots, slabs),
        out_shape=jax.ShapeDtypeStruct((2 * slabs, slots, 2, pieces, planes, LANES), F32),
        grid=(slots,),
        in_specs=[
            whole_block(levels, pltpu.SMEM),
            whole_block(scale, pltpu.SMEM),
            whole_block(tz),
            whole_block(ty),
            pl.BlockSpec((None, pieces, depth * rows, LANES), lambda k: (k // four, 0, 0, 0)),
        ],
        out_specs=anywhere,
        scratch_shapes=[
            pltpu.VMEM((2, depth, height), F32),
            pltpu.VMEM((slots, 2, pieces, depth, LANES), F32),
            pltpu.SemaphoreType.DMA((shots, slabs)),
            pltpu.SemaphoreType.DMA((2 * slabs,)),
            pltpu.SemaphoreType.DMA,
        ],
        compiler_params=params(has_side_effects=True),
    )(levels, scale, tz, ty, gathered)

    terms = returned.reshape(2 * half * pieces * planes, LANES)
    return pl.pallas_call(
        functools.partial(inverse_x, planes, pieces),
        out_shape=jax.ShapeDtypeStruct((planes, height, width), F32),
        grid=(planes,),
        in_specs=[whole_block(terms), whole_block(tx_back)],
        out_specs=pl.BlockSpec((1, height, width), lambda z: (z, 0, 0)),
        compiler_params=params(),
    )(terms, tx_back)


def solution(mesh):
    placed = (
        P("shot", "slab", None, None),
        P("shot", "slab", None, None),
        P("shot"),
        P(("slab", "shot"), None, None),
        P(),
        P(),
    )
    return jax.shard_map(
        on_device,
        mesh=mesh,
        in_specs=placed,
        out_specs=P(("slab", "shot"), None, None),
        check_vma=False,
    )
```

```python
import functools

import jax
import jax.numpy as jnp
import numpy as np
from jax import lax
from jax.experimental import pallas as pl
from jax.experimental.pallas import tpu as pltpu
from jax.sharding import PartitionSpec as P

STEP_SIZE = 0.25
EPSILON = 1e-06
LANES = 128
ROWS = 64
LAG = 3
BUFFERS = 4
AHEAD = 2
F32 = jnp.float32
BF16 = jnp.bfloat16
MESH = pl.DeviceIdType.MESH
VMEM_LIMIT = 60 * 1024 * 1024


def halves(x):
    high = x.astype(BF16)
    return high, (x - high.astype(F32)).astype(BF16)


def host_halves(table):
    table = table.astype(np.float32)
    high = table.astype(BF16)
    low = (table - high.astype(np.float32)).astype(BF16)
    return np.stack([high, low])


def dot3(a, b, dims=((1,), (0,))):
    product = functools.partial(
        lax.dot_general, dimension_numbers=(dims, ((), ())), preferred_element_type=F32
    )
    return product(a[0], b[0]) + (product(a[0], b[1]) + product(a[1], b[0]))


def circle(rows, columns, length):
    angle = (np.outer(rows, columns) % length) * (2.0 * np.pi / length)
    return np.cos(angle), np.sin(angle)


def x_table(parity, width):
    half = width // 2
    cosine, sine = circle(2 * np.arange(half // 2) + parity, np.arange(half), width)
    sine = -sine
    if parity == 0:
        sine[0] = 1.0 - 2.0 * (np.arange(half) % 2)
    return np.stack([cosine, sine], axis=1)


def reduce_forward(
    shots, slabs, sign_ref, size_ref, factor_ref, source_ref, recv_ref, model_ref, tx_ref, column_ref, g_ref, levels,
    acc, along_x, power_ref, shares, source_buf, recv_buf, model_buf, in_sem, chain_send, chain_recv,
    ex_send, ex_recv, own_sem, share_send, share_recv,
):
    shot = lax.axis_index("shot")
    slab = lax.axis_index("slab")
    local, height, width = source_ref.shape
    planes = model_ref.shape[0]
    half = width // 2
    pieces = height // LANES
    parts = height // ROWS
    chunks = local * parts
    groups = g_ref.shape[0]
    rows = along_x.shape[4]
    hops = (shots - 1 - shot, shot)
    last = shots - 1
    parity = jnp.where(shot == 0, 0, 1)
    me = parity * slabs + slab
    wedges = size_ref.shape[0]
    base = chunks * (1 + 4 * (LAG * shots + AHEAD) // chunks)

    def inputs(way, chunk):
        slot = lax.rem(chunk, BUFFERS)
        plane = chunk // parts
        span = pl.ds(pl.multiple_of(lax.rem(chunk, parts) * ROWS, ROWS), ROWS)
        return (
            pltpu.make_async_copy(
                source_ref.at[plane, span], source_buf.at[way, slot], in_sem.at[way, slot, 0]
            ),
            pltpu.make_async_copy(
                recv_ref.at[:, plane, span], recv_buf.at[way, slot], in_sem.at[way, slot, 1]
            ),
        )

    def own_model(way, chunk):
        slot = lax.rem(chunk, BUFFERS)
        plane = chunk // parts
        span = pl.ds(pl.multiple_of(lax.rem(chunk, parts) * ROWS, ROWS), ROWS)
        return pltpu.make_async_copy(
            model_ref.at[lax.rem(plane, planes), span], model_buf.at[way, slot], in_sem.at[way, slot, 2]
        )

    def owned(chunk):
        return chunk // parts // planes == shot

    def exchange(plane, piece, other):
        return pltpu.make_async_remote_copy(
            src_ref=along_x.at[plane, other, :, piece],
            dst_ref=g_ref.at[:, piece, pl.ds(pl.multiple_of((slab * local + plane) * rows, rows), rows)],
            send_sem=ex_send.at[other],
            recv_sem=ex_recv.at[slab],
            device_id=(shot, other),
            device_id_type=MESH,
        )

    def keep(plane, piece):
        return pltpu.make_async_copy(
            along_x.at[plane, slab, :, piece],
            g_ref.at[:, piece, pl.ds(pl.multiple_of((slab * local + plane) * rows, rows), rows)],
            own_sem,
        )

    def join(way, low, high):
        return low + high if way == 0 else low - high

    def share(source, to):
        return pltpu.make_async_remote_copy(
            src_ref=shares.at[source],
            dst_ref=shares.at[source],
            send_sem=share_send.at[to],
            recv_sem=share_recv.at[source],
            device_id=(to // slabs * last, lax.rem(to, slabs)),
            device_id_type=MESH,
        )

    def wedge_vectors():
        lane = lax.broadcasted_iota(jnp.int32, (1, LANES), 1)
        starts = jnp.zeros((1, LANES), jnp.int32)
        sizes = jnp.zeros((1, LANES), jnp.int32)
        factors = jnp.zeros((1, LANES), F32)
        start = 0
        for wedge in range(wedges):
            starts = jnp.where(lane == wedge, start, starts)
            sizes = jnp.where(lane == wedge, size_ref[wedge], sizes)
            factors = jnp.where(lane == wedge, factor_ref[wedge], factors)
            start = start + size_ref[wedge]
        return starts, sizes, factors

    def members_of(columns, starts, sizes):
        return jnp.where((columns >= starts) & (columns < starts + sizes), 1.0, 0.0)

    def mirrored(columns):
        return jnp.where(columns == 0, 0, width - columns)

    def offer_power():
        starts, sizes, _ = wedge_vectors()
        columns = column_ref[parity]
        paired = mirrored(columns)
        counted = members_of(columns, starts, sizes)
        counted = counted + jnp.where(paired == columns, 0.0, members_of(paired, starts, sizes))
        summed = jnp.sum(power_ref[...], axis=1, keepdims=True)
        own = jnp.sum(counted * summed, axis=0, keepdims=True)
        shares[me] = jnp.broadcast_to(own, shares.shape[1:])

        def give(offset, carry):
            share(me, lax.rem(me + offset, 2 * slabs)).start()
            return carry

        lax.fori_loop(1, 2 * slabs, give, 0)

    def take_levels():
        def take(offset, carry):
            other = lax.rem(me + offset, 2 * slabs)
            pltpu.make_async_copy(shares.at[other], shares.at[other], share_send.at[other]).wait()
            pltpu.make_async_copy(shares.at[other], shares.at[other], share_recv.at[other]).wait()
            return carry

        lax.fori_loop(1, 2 * slabs, take, 0)
        starts, sizes, factors = wedge_vectors()
        total = jnp.sum(shares[...], axis=0)[:1]
        heights = factors * jnp.sqrt(total / jnp.maximum(sizes, 1).astype(F32) + EPSILON)
        index = lax.broadcasted_iota(jnp.int32, (levels.shape[1], LANES), 0)
        columns = jnp.where(index == groups * (rows // 2), width // 2, 2 * (slab * groups * (rows // 2) + index) + parity)
        for side, picked in enumerate((columns, mirrored(columns))):
            level = jnp.sum(members_of(picked, starts, sizes) * heights, axis=1, keepdims=True)
            levels[side] = jnp.broadcast_to(level, levels.shape[1:])

    power_ref[...] = jnp.zeros_like(power_ref)
    levels[...] = jnp.zeros_like(levels)

    def step(t, carry):
        for way in range(2):
            count = t + base - LAG * hops[way]
            chunk = lax.rem(count, chunks)

            @pl.when((count >= base) & (count < base + chunks))
            def _():
                for copy in inputs(way, chunk):
                    copy.start()

                @pl.when(owned(chunk))
                def _():
                    own_model(way, chunk).start()

        for way in range(2):
            count = t - AHEAD + base - LAG * hops[way]
            chunk = lax.rem(count, chunks)

            @pl.when((count >= base) & (count < base + chunks))
            def _():
                slot = lax.rem(chunk, BUFFERS)
                rows_here = pl.ds(pl.multiple_of(chunk * ROWS, ROWS), ROWS)
                here = acc.at[way, rows_here]
                for copy in inputs(way, chunk):
                    copy.wait()
                encoded = jnp.zeros((ROWS, width), F32)
                for member in range(recv_ref.shape[0]):
                    encoded = encoded + sign_ref[member].astype(F32) * recv_buf[way, slot, member].astype(F32)
                part = -STEP_SIZE * (source_buf[way, slot].astype(F32) * encoded)
                part = join(way, part[:, :half], part[:, half:])

                @pl.when(hops[way] > 0)
                def _():
                    pltpu.make_async_copy(here, here, chain_recv.at[way, chunk]).wait()
                    acc[way, rows_here] = acc[way, rows_here] + part

                @pl.when(hops[way] == 0)
                def _():
                    acc[way, rows_here] = part

                @pl.when(owned(chunk))
                def _():
                    own_model(way, chunk).wait()
                    image = model_buf[way, slot].astype(F32)
                    acc[way, rows_here] = acc[way, rows_here] + join(way, image[:, :half], image[:, half:])

                @pl.when(hops[way] < last)
                def _():
                    pltpu.make_async_remote_copy(
                        src_ref=here,
                        dst_ref=here,
                        send_sem=chain_send.at[way],
                        recv_sem=chain_recv.at[way, chunk],
                        device_id=(shot - 1 + 2 * way, slab),
                        device_id_type=MESH,
                    ).start()

                per_piece = LANES // ROWS

                @pl.when((hops[way] == last) & (lax.rem(chunk, per_piece) == per_piece - 1))
                def _():
                    plane = chunk // parts
                    first = chunk // per_piece
                    piece = lax.rem(first, pieces)
                    summed = acc[way, pl.ds(pl.multiple_of(first * LANES, LANES), LANES)]
                    result = dot3((tx_ref[way, 0], tx_ref[way, 1]), halves(summed), ((1,), (1,)))
                    power_ref[...] = power_ref[...] + result * result
                    along_x[plane, :, :, piece] = result.reshape(slabs, groups, rows, LANES)

                    def send(offset, carry):
                        exchange(plane, piece, lax.rem(slab + offset, slabs)).start()
                        return carry

                    lax.fori_loop(1, slabs, send, 0)
                    keep(plane, piece).start()

        return carry

    lax.fori_loop(0, chunks + LAG * last + AHEAD, step, 0)

    pl.when((shot == 0) | (shot == last))(offer_power)

    for way in range(2):

        @pl.when(hops[way] < last)
        def _():
            sent = acc.at[way]
            pltpu.make_async_copy(sent, sent, chain_send.at[way]).wait()

    @pl.when((shot == 0) | (shot == last))
    def _():
        def part_of(other):
            return g_ref.at[:, :, pl.ds(pl.multiple_of(other * local * rows, rows), local * rows)]

        def finish(offset, carry):
            other = lax.rem(slab + offset, slabs)
            piece = part_of(other)
            pltpu.make_async_copy(piece, piece, ex_send.at[other]).wait()
            pltpu.make_async_copy(piece, piece, ex_recv.at[other]).wait()
            return carry

        lax.fori_loop(1, slabs, finish, 0)
        mine = part_of(slab)
        pltpu.make_async_copy(mine, mine, own_sem).wait()
        take_levels()


def shrink_back(
    shots, slabs, x_width, level_ref, tz_ref, ty_ref, g_ref, r_ref, held, out, send_sem, recv_sem, own_sem
):
    step = pl.program_id(0)
    slot = pl.num_programs(0) - 1 - step
    shot = lax.axis_index("shot")
    slab = lax.axis_index("slab")
    slots, _, pieces, depth, _ = out.shape
    width = pieces * LANES
    planes = r_ref.shape[4]
    rows = g_ref.shape[1] // depth
    devices = shots * slabs
    last = shots - 1
    end = (shot == 0) | (shot == last)
    me = jnp.where(shot == 0, 0, slabs) + slab

    def along_y(re, im, sign):
        result = dot3(halves(jnp.concatenate([re, im], axis=0)), (ty_ref[0], ty_ref[1]))
        with_cos, with_sin = result[:, :width], result[:, width:]
        return (
            with_cos[:depth] + sign * with_sin[depth:],
            with_cos[depth:] - sign * with_sin[:depth],
        )

    def along_z(re, im, sign):
        result = dot3((tz_ref[0], tz_ref[1]), halves(jnp.concatenate([re, im], axis=1)))
        with_cos, with_sin = result[:depth], result[depth:]
        return (
            with_cos[:, :width] + sign * with_sin[:, width:],
            with_cos[:, width:] - sign * with_sin[:, :width],
        )

    def target(index):
        far = index // slabs
        to_shot = jnp.where(shot == 0, last - far, far)
        to_slab = lax.rem(slab + index, slabs)
        return to_shot, to_slab

    def part(to_shot, to_slab):
        first = to_slab * (shots * planes) + to_shot * planes
        return out.at[slot, :, :, pl.ds(pl.multiple_of(first, planes), planes)]

    @pl.when(end)
    def _():
        packed = (shot == 0) & (slab == 0) & (slot == 0)
        row = lax.rem(slot, rows // 2)

        def spread(first):
            return jnp.concatenate(
                [g_ref[piece, pl.ds(first, depth, stride=rows), :] for piece in range(pieces)], axis=1
            )

        def column(which, carry):
            re = spread(row + which * (rows // 2))
            im = jnp.where(packed, 0.0, spread(row + rows // 2))
            re, im = along_z(*along_y(re, im, 1.0), 1.0)

            index = slot + which * slots
            magnitude = jnp.sqrt(re * re + im * im)
            total = 0.0
            for side in range(2):
                level = level_ref[side, pl.ds(index, 1)]
                total = total + jnp.maximum(magnitude - level, 0.0) / jnp.maximum(magnitude, level)
            total = total * (jnp.where(packed, 0.5, 1.0) * (1.0 / (depth * width * x_width)))
            re, im = re * total, im * total

            @pl.when(which == 0)
            def _():
                held[0] = re
                held[1] = im

            @pl.when(which == 1)
            def _():
                held[0] = held[0] - im
                held[1] = held[1] + re

            return carry

        lax.fori_loop(0, jnp.where(packed, 2, 1), column, 0)
        re, im = along_y(*along_z(held[0], held[1], -1.0), -1.0)
        for piece in range(pieces):
            span = slice(piece * LANES, (piece + 1) * LANES)
            out[slot, 0, piece] = re[:, span]
            out[slot, 1, piece] = im[:, span]

        def send(index, carry):
            to_shot, to_slab = target(index)

            @pl.when((to_shot != shot) | (to_slab != slab))
            def _():
                pltpu.make_async_remote_copy(
                    src_ref=part(to_shot, to_slab),
                    dst_ref=r_ref.at[me, slot],
                    send_sem=send_sem.at[to_shot, to_slab],
                    recv_sem=recv_sem.at[me],
                    device_id=(to_shot, to_slab),
                    device_id_type=MESH,
                ).start()

            return carry

        lax.fori_loop(0, devices, send, 0)
        pltpu.make_async_copy(part(shot, slab), r_ref.at[me, slot], own_sem).start()

    @pl.when(step == slots - 1)
    def _():
        @pl.when(end)
        def _():
            def sent(index, carry):
                to_shot, to_slab = target(index)

                @pl.when((to_shot != shot) | (to_slab != slab))
                def _():
                    pltpu.make_async_copy(r_ref.at[0], r_ref.at[0], send_sem.at[to_shot, to_slab]).wait()

                return carry

            lax.fori_loop(0, devices, sent, 0)
            pltpu.make_async_copy(r_ref.at[me], r_ref.at[me], own_sem).wait()

        def arrived(index, carry):
            @pl.when(jnp.logical_not(end) | (index != me))
            def _():
                pltpu.make_async_copy(r_ref.at[index], r_ref.at[index], recv_sem.at[index]).wait()

            return carry

        lax.fori_loop(0, 2 * slabs, arrived, 0)


def inverse_x(planes, pieces, r_ref, tx_ref, out_ref):
    plane = pl.program_id(0)
    count = tx_ref.shape[2]

    def side(parity):
        pitch = pieces * planes
        terms = jnp.concatenate(
            [
                r_ref[pl.ds(parity * count * pitch + piece * planes + plane, count, stride=pitch), :]
                for piece in range(pieces)
            ],
            axis=1,
        )
        return dot3(halves(terms), (tx_ref[parity, 0], tx_ref[parity, 1]), ((0,), (0,)))

    even, odd = side(0), side(1)
    half = even.shape[1]
    out_ref[0, :, :half] = even + odd
    out_ref[0, :, half:] = even - odd


def whole_block(array, memory_space=None):
    if memory_space is not None:
        return pl.BlockSpec(memory_space=memory_space)
    zeros = (0,) * array.ndim
    return pl.BlockSpec(array.shape, lambda *_: zeros)


def on_device(source_field, receiver_fields, weights, model, wedge_sizes, wedge_scales):
    shots = lax.axis_size("shot")
    slabs = lax.axis_size("slab")
    shot = lax.axis_index("shot")
    slab = lax.axis_index("slab")
    devices = shots * slabs
    members, local, height, width = receiver_fields.shape
    planes = model.shape[0]
    depth = local * slabs
    half = width // 2
    slots = half // 2 // slabs
    four = min(4, slots)
    groups, rows = slots // four, 2 * four
    pieces = height // LANES
    chunks = local * (height // ROWS)
    params = functools.partial(pltpu.CompilerParams, vmem_limit_bytes=VMEM_LIMIT)

    tables = [x_table(parity, width).reshape(slabs, groups, four, 2, half) for parity in range(2)]
    tx = np.stack([host_halves(t.transpose(0, 1, 3, 2, 4).reshape(half, half)) for t in tables])
    tx_back = np.stack([host_halves(t.reshape(half, half)) for t in tables])
    ty = host_halves(np.concatenate(circle(np.arange(height), np.arange(height), height), axis=1))
    tz = host_halves(np.concatenate(circle(np.arange(depth), np.arange(depth), depth), axis=0))
    tx, tx_back, ty, tz = (jnp.asarray(table) for table in (tx, tx_back, ty, tz))

    row_slots = (
        np.arange(slabs)[:, None, None, None] * slots
        + np.arange(groups)[:, None, None] * four
        + np.zeros((2, 1), np.int32)
        + np.arange(four)
    ).reshape(-1)
    row_columns = 2 * row_slots + np.arange(2)[:, None]
    row_columns[0, four] = half
    row_columns = np.broadcast_to(row_columns[:, :, None], (2, half, LANES)).astype(np.int32)
    row_columns = jnp.asarray(row_columns)

    anywhere = pl.BlockSpec(memory_space=pl.ANY)
    gathered, levels = pl.pallas_call(
        functools.partial(reduce_forward, shots, slabs),
        out_shape=(
            jax.ShapeDtypeStruct((groups, pieces, depth * rows, LANES), F32),
            jax.ShapeDtypeStruct((2, slots // 8 * 8 + 8, height), F32),
        ),
        in_specs=[
            pl.BlockSpec(memory_space=pltpu.SMEM),
            pl.BlockSpec(memory_space=pltpu.SMEM),
            pl.BlockSpec(memory_space=pltpu.SMEM),
            anywhere,
            anywhere,
            anywhere,
            pl.BlockSpec(memory_space=pltpu.VMEM),
            pl.BlockSpec(memory_space=pltpu.VMEM),
        ],
        out_specs=(anywhere, pl.BlockSpec(memory_space=pltpu.VMEM)),
        scratch_shapes=[
            pltpu.VMEM((2, local * height, half), F32),
            pltpu.VMEM((local, slabs, groups, pieces, rows, LANES), F32),
            pltpu.VMEM((half, LANES), F32),
            pltpu.VMEM((2 * slabs, 8, LANES), F32),
            pltpu.VMEM((2, BUFFERS, ROWS, width), BF16),
            pltpu.VMEM((2, BUFFERS, members, ROWS, width), BF16),
            pltpu.VMEM((2, BUFFERS, ROWS, width), BF16),
            pltpu.SemaphoreType.DMA((2, BUFFERS, 3)),
            pltpu.SemaphoreType.DMA((2,)),
            pltpu.SemaphoreType.DMA((2, chunks)),
            pltpu.SemaphoreType.DMA((slabs,)),
            pltpu.SemaphoreType.DMA((slabs,)),
            pltpu.SemaphoreType.DMA,
            pltpu.SemaphoreType.DMA((2 * slabs,)),
            pltpu.SemaphoreType.DMA((2 * slabs,)),
        ],
        compiler_params=params(has_side_effects=True),
    )(weights, wedge_sizes, wedge_scales, source_field[0], receiver_fields, model, tx, row_columns)

    returned = pl.pallas_call(
        functools.partial(shrink_back, shots, slabs, width),
        out_shape=jax.ShapeDtypeStruct((2 * slabs, slots, 2, pieces, planes, LANES), F32),
        grid=(slots,),
        in_specs=[
            whole_block(levels),
            whole_block(tz),
            whole_block(ty),
            pl.BlockSpec((None, pieces, depth * rows, LANES), lambda k: ((slots - 1 - k) // four, 0, 0, 0)),
        ],
        out_specs=anywhere,
        scratch_shapes=[
            pltpu.VMEM((2, depth, height), F32),
            pltpu.VMEM((slots, 2, pieces, depth, LANES), F32),
            pltpu.SemaphoreType.DMA((shots, slabs)),
            pltpu.SemaphoreType.DMA((2 * slabs,)),
            pltpu.SemaphoreType.DMA,
        ],
        compiler_params=params(has_side_effects=True),
    )(levels, tz, ty, gathered)

    terms = returned.reshape(2 * half * pieces * planes, LANES)
    return pl.pallas_call(
        functools.partial(inverse_x, planes, pieces),
        out_shape=jax.ShapeDtypeStruct((planes, height, width), F32),
        grid=(planes,),
        in_specs=[whole_block(terms), whole_block(tx_back)],
        out_specs=pl.BlockSpec((1, height, width), lambda z: (z, 0, 0)),
        compiler_params=params(),
    )(terms, tx_back)


def solution(mesh):
    placed = (
        P("shot", "slab", None, None),
        P("shot", "slab", None, None),
        P("shot"),
        P(("slab", "shot"), None, None),
        P(),
        P(),
    )
    return jax.shard_map(
        on_device,
        mesh=mesh,
        in_specs=placed,
        out_specs=P(("slab", "shot"), None, None),
        check_vma=False,
    )
```

```python
import functools

import jax
import jax.numpy as jnp
import numpy as np
from jax import lax
from jax.experimental import pallas as pl
from jax.experimental.pallas import tpu as pltpu
from jax.sharding import PartitionSpec as P

STEP_SIZE = 0.25
EPSILON = 1e-06
LANES = 128
ROWS = 64
LAG = 3
BUFFERS = 4
AHEAD = 2
F32 = jnp.float32
BF16 = jnp.bfloat16
MESH = pl.DeviceIdType.MESH
VMEM_LIMIT = 60 * 1024 * 1024


def halves(x):
    high = x.astype(BF16)
    return high, (x - high.astype(F32)).astype(BF16)


def host_halves(table):
    table = table.astype(np.float32)
    high = table.astype(BF16)
    low = (table - high.astype(np.float32)).astype(BF16)
    return np.stack([high, low])


def dot3(a, b, dims=((1,), (0,))):
    product = functools.partial(
        lax.dot_general, dimension_numbers=(dims, ((), ())), preferred_element_type=F32
    )
    return product(a[0], b[0]) + (product(a[0], b[1]) + product(a[1], b[0]))


def circle(rows, columns, length):
    angle = (np.outer(rows, columns) % length) * (2.0 * np.pi / length)
    return np.cos(angle), np.sin(angle)


def x_table(parity, width):
    half = width // 2
    cosine, sine = circle(2 * np.arange(half // 2) + parity, np.arange(half), width)
    sine = -sine
    if parity == 0:
        sine[0] = 1.0 - 2.0 * (np.arange(half) % 2)
    return np.stack([cosine, sine], axis=1)


def reduce_forward(
    shots, slabs, sign_ref, size_ref, factor_ref, source_ref, recv_ref, model_ref, tx_ref, column_ref, g_ref, levels,
    acc, along_x, power_ref, shares, source_buf, recv_buf, model_buf, in_sem, chain_send, chain_recv,
    ex_send, ex_recv, own_sem, share_send, share_recv,
):
    shot = lax.axis_index("shot")
    slab = lax.axis_index("slab")
    local, height, width = source_ref.shape
    planes = model_ref.shape[0]
    half = width // 2
    pieces = height // LANES
    parts = height // ROWS
    chunks = local * parts
    groups = g_ref.shape[0]
    rows = along_x.shape[4]
    hops = (shots - 1 - shot, shot)
    last = shots - 1
    parity = jnp.where(shot == 0, 0, 1)
    me = parity * slabs + slab
    wedges = size_ref.shape[0]
    base = chunks * (1 + 4 * (LAG * shots + AHEAD) // chunks)

    def inputs(way, chunk):
        slot = lax.rem(chunk, BUFFERS)
        plane = chunk // parts
        span = pl.ds(pl.multiple_of(lax.rem(chunk, parts) * ROWS, ROWS), ROWS)
        return (
            pltpu.make_async_copy(
                source_ref.at[plane, span], source_buf.at[way, slot], in_sem.at[way, slot, 0]
            ),
            pltpu.make_async_copy(
                recv_ref.at[:, plane, span], recv_buf.at[way, slot], in_sem.at[way, slot, 1]
            ),
        )

    def own_model(way, chunk):
        slot = lax.rem(chunk, BUFFERS)
        plane = chunk // parts
        span = pl.ds(pl.multiple_of(lax.rem(chunk, parts) * ROWS, ROWS), ROWS)
        return pltpu.make_async_copy(
            model_ref.at[lax.rem(plane, planes), span], model_buf.at[way, slot], in_sem.at[way, slot, 2]
        )

    def owned(chunk):
        return chunk // parts // planes == shot

    def exchange(plane, piece, other):
        return pltpu.make_async_remote_copy(
            src_ref=along_x.at[plane, other, :, piece],
            dst_ref=g_ref.at[:, piece, pl.ds(pl.multiple_of((slab * local + plane) * rows, rows), rows)],
            send_sem=ex_send.at[other],
            recv_sem=ex_recv.at[slab],
            device_id=(shot, other),
            device_id_type=MESH,
        )

    def keep(plane, piece):
        return pltpu.make_async_copy(
            along_x.at[plane, slab, :, piece],
            g_ref.at[:, piece, pl.ds(pl.multiple_of((slab * local + plane) * rows, rows), rows)],
            own_sem,
        )

    def join(way, low, high):
        return low + high if way == 0 else low - high

    def share(source, to):
        return pltpu.make_async_remote_copy(
            src_ref=shares.at[source],
            dst_ref=shares.at[source],
            send_sem=share_send.at[to],
            recv_sem=share_recv.at[source],
            device_id=(to // slabs * last, lax.rem(to, slabs)),
            device_id_type=MESH,
        )

    def wedge_vectors():
        lane = lax.broadcasted_iota(jnp.int32, (1, LANES), 1)
        starts = jnp.zeros((1, LANES), jnp.int32)
        sizes = jnp.zeros((1, LANES), jnp.int32)
        factors = jnp.zeros((1, LANES), F32)
        start = 0
        for wedge in range(wedges):
            starts = jnp.where(lane == wedge, start, starts)
            sizes = jnp.where(lane == wedge, size_ref[wedge], sizes)
            factors = jnp.where(lane == wedge, factor_ref[wedge], factors)
            start = start + size_ref[wedge]
        return starts, sizes, factors

    def members_of(columns, starts, sizes):
        return jnp.where((columns >= starts) & (columns < starts + sizes), 1.0, 0.0)

    def mirrored(columns):
        return jnp.where(columns == 0, 0, width - columns)

    def offer_power():
        starts, sizes, _ = wedge_vectors()
        columns = column_ref[parity]
        paired = mirrored(columns)
        counted = members_of(columns, starts, sizes)
        counted = counted + jnp.where(paired == columns, 0.0, members_of(paired, starts, sizes))
        summed = jnp.sum(power_ref[...], axis=1, keepdims=True)
        own = jnp.sum(counted * summed, axis=0, keepdims=True)
        shares[me] = jnp.broadcast_to(own, shares.shape[1:])

        def give(offset, carry):
            share(me, lax.rem(me + offset, 2 * slabs)).start()
            return carry

        lax.fori_loop(1, 2 * slabs, give, 0)

    def take_levels():
        def take(offset, carry):
            other = lax.rem(me + offset, 2 * slabs)
            pltpu.make_async_copy(shares.at[other], shares.at[other], share_send.at[other]).wait()
            pltpu.make_async_copy(shares.at[other], shares.at[other], share_recv.at[other]).wait()
            return carry

        lax.fori_loop(1, 2 * slabs, take, 0)
        starts, sizes, factors = wedge_vectors()
        total = jnp.sum(shares[...], axis=0)[:1]
        heights = factors * jnp.sqrt(total / jnp.maximum(sizes, 1).astype(F32) + EPSILON)
        index = lax.broadcasted_iota(jnp.int32, (levels.shape[1], LANES), 0)
        columns = jnp.where(index == groups * (rows // 2), width // 2, 2 * (slab * groups * (rows // 2) + index) + parity)
        for side, picked in enumerate((columns, mirrored(columns))):
            level = jnp.sum(members_of(picked, starts, sizes) * heights, axis=1, keepdims=True)
            levels[side] = jnp.broadcast_to(level, levels.shape[1:])

    power_ref[...] = jnp.zeros_like(power_ref)
    levels[...] = jnp.zeros_like(levels)

    def fetch(t):
        for way in range(2):
            count = t + base - LAG * hops[way]
            chunk = lax.rem(count, chunks)

            @pl.when((count >= base) & (count < base + chunks))
            def _():
                for copy in inputs(way, chunk):
                    copy.start()

                @pl.when(owned(chunk))
                def _():
                    own_model(way, chunk).start()

    def step(t, carry):
        fetch(t)
        for way in range(2):
            count = t - AHEAD + base - LAG * hops[way]
            chunk = lax.rem(count, chunks)

            @pl.when((count >= base) & (count < base + chunks))
            def _():
                slot = lax.rem(chunk, BUFFERS)
                rows_here = pl.ds(pl.multiple_of(chunk * ROWS, ROWS), ROWS)
                here = acc.at[way, rows_here]
                for copy in inputs(way, chunk):
                    copy.wait()
                encoded = jnp.zeros((ROWS, width), F32)
                for member in range(recv_ref.shape[0]):
                    encoded = encoded + sign_ref[member].astype(F32) * recv_buf[way, slot, member].astype(F32)
                part = -STEP_SIZE * (source_buf[way, slot].astype(F32) * encoded)
                part = join(way, part[:, :half], part[:, half:])

                @pl.when(hops[way] > 0)
                def _():
                    pltpu.make_async_copy(here, here, chain_recv.at[way, chunk]).wait()
                    acc[way, rows_here] = acc[way, rows_here] + part

                @pl.when(hops[way] == 0)
                def _():
                    acc[way, rows_here] = part

                @pl.when(owned(chunk))
                def _():
                    own_model(way, chunk).wait()
                    image = model_buf[way, slot].astype(F32)
                    acc[way, rows_here] = acc[way, rows_here] + join(way, image[:, :half], image[:, half:])

                @pl.when(hops[way] < last)
                def _():
                    pltpu.make_async_remote_copy(
                        src_ref=here,
                        dst_ref=here,
                        send_sem=chain_send.at[way],
                        recv_sem=chain_recv.at[way, chunk],
                        device_id=(shot - 1 + 2 * way, slab),
                        device_id_type=MESH,
                    ).start()

                per_piece = LANES // ROWS

                @pl.when((hops[way] == last) & (lax.rem(chunk, per_piece) == per_piece - 1))
                def _():
                    plane = chunk // parts
                    first = chunk // per_piece
                    piece = lax.rem(first, pieces)
                    summed = acc[way, pl.ds(pl.multiple_of(first * LANES, LANES), LANES)]
                    result = dot3((tx_ref[way, 0], tx_ref[way, 1]), halves(summed), ((1,), (1,)))
                    power_ref[...] = power_ref[...] + result * result
                    along_x[plane, :, :, piece] = result.reshape(slabs, groups, rows, LANES)

                    def send(offset, carry):
                        exchange(plane, piece, lax.rem(slab + offset, slabs)).start()
                        return carry

                    lax.fori_loop(1, slabs, send, 0)
                    keep(plane, piece).start()

        return carry

    end = (shot == 0) | (shot == last)
    barrier = pltpu.get_barrier_semaphore()

    def greet(to_shot, to_slab):
        pl.semaphore_signal(barrier, inc=1, device_id=(to_shot, to_slab), device_id_type=MESH)

    @pl.when(shot > 0)
    def _():
        greet(shot - 1, slab)

    @pl.when(shot < last)
    def _():
        greet(shot + 1, slab)

    @pl.when(end)
    def _():
        def greet_end(offset, carry):
            other = lax.rem(me + offset, 2 * slabs)
            greet(other // slabs * last, lax.rem(other, slabs))
            return carry

        lax.fori_loop(1, 2 * slabs, greet_end, 0)

    for t in range(AHEAD):
        fetch(t)

    @pl.when(end)
    def _():
        pl.semaphore_wait(barrier, 2 * slabs)

    @pl.when(jnp.logical_not(end))
    def _():
        pl.semaphore_wait(barrier, 2)

    lax.fori_loop(AHEAD, chunks + LAG * last + AHEAD, step, 0)

    pl.when(end)(offer_power)

    for way in range(2):

        @pl.when(hops[way] < last)
        def _():
            sent = acc.at[way]
            pltpu.make_async_copy(sent, sent, chain_send.at[way]).wait()

    @pl.when(end)
    def _():
        def part_of(other):
            return g_ref.at[:, :, pl.ds(pl.multiple_of(other * local * rows, rows), local * rows)]

        def finish(offset, carry):
            other = lax.rem(slab + offset, slabs)
            piece = part_of(other)
            pltpu.make_async_copy(piece, piece, ex_send.at[other]).wait()
            pltpu.make_async_copy(piece, piece, ex_recv.at[other]).wait()
            return carry

        lax.fori_loop(1, slabs, finish, 0)
        mine = part_of(slab)
        pltpu.make_async_copy(mine, mine, own_sem).wait()
        take_levels()


def shrink_back(
    shots, slabs, x_width, level_ref, tz_ref, ty_ref, g_ref, r_ref, held, out, send_sem, recv_sem, own_sem
):
    step = pl.program_id(0)
    slot = pl.num_programs(0) - 1 - step
    shot = lax.axis_index("shot")
    slab = lax.axis_index("slab")
    slots, _, pieces, depth, _ = out.shape
    width = pieces * LANES
    planes = r_ref.shape[4]
    rows = g_ref.shape[1] // depth
    devices = shots * slabs
    last = shots - 1
    end = (shot == 0) | (shot == last)
    me = jnp.where(shot == 0, 0, slabs) + slab

    def along_y(re, im, sign):
        result = dot3(halves(jnp.concatenate([re, im], axis=0)), (ty_ref[0], ty_ref[1]))
        with_cos, with_sin = result[:, :width], result[:, width:]
        return (
            with_cos[:depth] + sign * with_sin[depth:],
            with_cos[depth:] - sign * with_sin[:depth],
        )

    def along_z(re, im, sign):
        result = dot3((tz_ref[0], tz_ref[1]), halves(jnp.concatenate([re, im], axis=1)))
        with_cos, with_sin = result[:depth], result[depth:]
        return (
            with_cos[:, :width] + sign * with_sin[:, width:],
            with_cos[:, width:] - sign * with_sin[:, :width],
        )

    def target(index):
        far = index // slabs
        to_shot = jnp.where(shot == 0, last - far, far)
        to_slab = lax.rem(slab + index, slabs)
        return to_shot, to_slab

    def part(to_shot, to_slab):
        first = to_slab * (shots * planes) + to_shot * planes
        return out.at[slot, :, :, pl.ds(pl.multiple_of(first, planes), planes)]

    barrier = pltpu.get_barrier_semaphore()

    @pl.when(step == 0)
    def _():
        def greet(index, carry):
            to_shot, to_slab = target(index)
            met = end | (to_shot == 0) | (to_shot == last)

            @pl.when(met & ((to_shot != shot) | (to_slab != slab)))
            def _():
                pl.semaphore_signal(barrier, inc=1, device_id=(to_shot, to_slab), device_id_type=MESH)

            return carry

        lax.fori_loop(0, devices, greet, 0)

    @pl.when(end)
    def _():
        packed = (shot == 0) & (slab == 0) & (slot == 0)
        row = lax.rem(slot, rows // 2)

        def spread(first):
            return jnp.concatenate(
                [g_ref[piece, pl.ds(first, depth, stride=rows), :] for piece in range(pieces)], axis=1
            )

        def column(which, carry):
            re = spread(row + which * (rows // 2))
            im = jnp.where(packed, 0.0, spread(row + rows // 2))
            re, im = along_z(*along_y(re, im, 1.0), 1.0)

            index = slot + which * slots
            magnitude = jnp.sqrt(re * re + im * im)
            total = 0.0
            for side in range(2):
                level = level_ref[side, pl.ds(index, 1)]
                total = total + jnp.maximum(magnitude - level, 0.0) / jnp.maximum(magnitude, level)
            total = total * (jnp.where(packed, 0.5, 1.0) * (1.0 / (depth * width * x_width)))
            re, im = re * total, im * total

            @pl.when(which == 0)
            def _():
                held[0] = re
                held[1] = im

            @pl.when(which == 1)
            def _():
                held[0] = held[0] - im
                held[1] = held[1] + re

            return carry

        lax.fori_loop(0, jnp.where(packed, 2, 1), column, 0)
        re, im = along_y(*along_z(held[0], held[1], -1.0), -1.0)
        for piece in range(pieces):
            span = slice(piece * LANES, (piece + 1) * LANES)
            out[slot, 0, piece] = re[:, span]
            out[slot, 1, piece] = im[:, span]

    @pl.when((step == 0) & end)
    def _():
        pl.semaphore_wait(barrier, devices - 1)

    @pl.when((step == 0) & jnp.logical_not(end))
    def _():
        pl.semaphore_wait(barrier, 2 * slabs)

    @pl.when(end)
    def _():
        def send(index, carry):
            to_shot, to_slab = target(index)

            @pl.when((to_shot != shot) | (to_slab != slab))
            def _():
                pltpu.make_async_remote_copy(
                    src_ref=part(to_shot, to_slab),
                    dst_ref=r_ref.at[me, slot],
                    send_sem=send_sem.at[to_shot, to_slab],
                    recv_sem=recv_sem.at[me],
                    device_id=(to_shot, to_slab),
                    device_id_type=MESH,
                ).start()

            return carry

        lax.fori_loop(0, devices, send, 0)
        pltpu.make_async_copy(part(shot, slab), r_ref.at[me, slot], own_sem).start()

    @pl.when(step == slots - 1)
    def _():
        @pl.when(end)
        def _():
            def sent(index, carry):
                to_shot, to_slab = target(index)

                @pl.when((to_shot != shot) | (to_slab != slab))
                def _():
                    pltpu.make_async_copy(r_ref.at[0], r_ref.at[0], send_sem.at[to_shot, to_slab]).wait()

                return carry

            lax.fori_loop(0, devices, sent, 0)
            pltpu.make_async_copy(r_ref.at[me], r_ref.at[me], own_sem).wait()

        def arrived(index, carry):
            @pl.when(jnp.logical_not(end) | (index != me))
            def _():
                pltpu.make_async_copy(r_ref.at[index], r_ref.at[index], recv_sem.at[index]).wait()

            return carry

        lax.fori_loop(0, 2 * slabs, arrived, 0)


def inverse_x(planes, pieces, r_ref, tx_ref, out_ref):
    plane = pl.program_id(0)
    count = tx_ref.shape[2]

    def side(parity):
        pitch = pieces * planes
        terms = jnp.concatenate(
            [
                r_ref[pl.ds(parity * count * pitch + piece * planes + plane, count, stride=pitch), :]
                for piece in range(pieces)
            ],
            axis=1,
        )
        return dot3(halves(terms), (tx_ref[parity, 0], tx_ref[parity, 1]), ((0,), (0,)))

    even, odd = side(0), side(1)
    half = even.shape[1]
    out_ref[0, :, :half] = even + odd
    out_ref[0, :, half:] = even - odd


def whole_block(array, memory_space=None):
    if memory_space is not None:
        return pl.BlockSpec(memory_space=memory_space)
    zeros = (0,) * array.ndim
    return pl.BlockSpec(array.shape, lambda *_: zeros)


def on_device(source_field, receiver_fields, weights, model, wedge_sizes, wedge_scales):
    shots = lax.axis_size("shot")
    slabs = lax.axis_size("slab")
    shot = lax.axis_index("shot")
    slab = lax.axis_index("slab")
    devices = shots * slabs
    members, local, height, width = receiver_fields.shape
    planes = model.shape[0]
    depth = local * slabs
    half = width // 2
    slots = half // 2 // slabs
    four = min(4, slots)
    groups, rows = slots // four, 2 * four
    pieces = height // LANES
    chunks = local * (height // ROWS)
    params = functools.partial(pltpu.CompilerParams, vmem_limit_bytes=VMEM_LIMIT)

    tables = [x_table(parity, width).reshape(slabs, groups, four, 2, half) for parity in range(2)]
    tx = np.stack([host_halves(t.transpose(0, 1, 3, 2, 4).reshape(half, half)) for t in tables])
    tx_back = np.stack([host_halves(t.reshape(half, half)) for t in tables])
    ty = host_halves(np.concatenate(circle(np.arange(height), np.arange(height), height), axis=1))
    tz = host_halves(np.concatenate(circle(np.arange(depth), np.arange(depth), depth), axis=0))
    tx, tx_back, ty, tz = (jnp.asarray(table) for table in (tx, tx_back, ty, tz))

    row_slots = (
        np.arange(slabs)[:, None, None, None] * slots
        + np.arange(groups)[:, None, None] * four
        + np.zeros((2, 1), np.int32)
        + np.arange(four)
    ).reshape(-1)
    row_columns = 2 * row_slots + np.arange(2)[:, None]
    row_columns[0, four] = half
    row_columns = np.broadcast_to(row_columns[:, :, None], (2, half, LANES)).astype(np.int32)
    row_columns = jnp.asarray(row_columns)

    anywhere = pl.BlockSpec(memory_space=pl.ANY)
    gathered, levels = pl.pallas_call(
        functools.partial(reduce_forward, shots, slabs),
        out_shape=(
            jax.ShapeDtypeStruct((groups, pieces, depth * rows, LANES), F32),
            jax.ShapeDtypeStruct((2, slots // 8 * 8 + 8, height), F32),
        ),
        in_specs=[
            pl.BlockSpec(memory_space=pltpu.SMEM),
            pl.BlockSpec(memory_space=pltpu.SMEM),
            pl.BlockSpec(memory_space=pltpu.SMEM),
            anywhere,
            anywhere,
            anywhere,
            pl.BlockSpec(memory_space=pltpu.VMEM),
            pl.BlockSpec(memory_space=pltpu.VMEM),
        ],
        out_specs=(anywhere, pl.BlockSpec(memory_space=pltpu.VMEM)),
        scratch_shapes=[
            pltpu.VMEM((2, local * height, half), F32),
            pltpu.VMEM((local, slabs, groups, pieces, rows, LANES), F32),
            pltpu.VMEM((half, LANES), F32),
            pltpu.VMEM((2 * slabs, 8, LANES), F32),
            pltpu.VMEM((2, BUFFERS, ROWS, width), BF16),
            pltpu.VMEM((2, BUFFERS, members, ROWS, width), BF16),
            pltpu.VMEM((2, BUFFERS, ROWS, width), BF16),
            pltpu.SemaphoreType.DMA((2, BUFFERS, 3)),
            pltpu.SemaphoreType.DMA((2,)),
            pltpu.SemaphoreType.DMA((2, chunks)),
            pltpu.SemaphoreType.DMA((slabs,)),
            pltpu.SemaphoreType.DMA((slabs,)),
            pltpu.SemaphoreType.DMA,
            pltpu.SemaphoreType.DMA((2 * slabs,)),
            pltpu.SemaphoreType.DMA((2 * slabs,)),
        ],
        compiler_params=params(collective_id=0, has_side_effects=True),
    )(weights, wedge_sizes, wedge_scales, source_field[0], receiver_fields, model, tx, row_columns)

    returned = pl.pallas_call(
        functools.partial(shrink_back, shots, slabs, width),
        out_shape=jax.ShapeDtypeStruct((2 * slabs, slots, 2, pieces, planes, LANES), F32),
        grid=(slots,),
        in_specs=[
            whole_block(levels),
            whole_block(tz),
            whole_block(ty),
            pl.BlockSpec((None, pieces, depth * rows, LANES), lambda k: ((slots - 1 - k) // four, 0, 0, 0)),
        ],
        out_specs=anywhere,
        scratch_shapes=[
            pltpu.VMEM((2, depth, height), F32),
            pltpu.VMEM((slots, 2, pieces, depth, LANES), F32),
            pltpu.SemaphoreType.DMA((shots, slabs)),
            pltpu.SemaphoreType.DMA((2 * slabs,)),
            pltpu.SemaphoreType.DMA,
        ],
        compiler_params=params(collective_id=1, has_side_effects=True),
    )(levels, tz, ty, gathered)

    terms = returned.reshape(2 * half * pieces * planes, LANES)
    return pl.pallas_call(
        functools.partial(inverse_x, planes, pieces),
        out_shape=jax.ShapeDtypeStruct((planes, height, width), F32),
        grid=(planes,),
        in_specs=[whole_block(terms), whole_block(tx_back)],
        out_specs=pl.BlockSpec((1, height, width), lambda z: (z, 0, 0)),
        compiler_params=params(),
    )(terms, tx_back)


def solution(mesh):
    placed = (
        P("shot", "slab", None, None),
        P("shot", "slab", None, None),
        P("shot"),
        P(("slab", "shot"), None, None),
        P(),
        P(),
    )
    return jax.shard_map(
        on_device,
        mesh=mesh,
        in_specs=placed,
        out_specs=P(("slab", "shot"), None, None),
        check_vma=False,
    )
```

```python
import functools
import math

import jax
import jax.numpy as jnp
import numpy as np
from jax import lax
from jax.experimental import pallas as pl
from jax.experimental.pallas import tpu as pltpu
from jax.sharding import PartitionSpec as P

STEP_SIZE = 0.25
EPSILON = 1e-06
LANES = 128
ROWS = 64
LAG = 3
BUFFERS = 4
AHEAD = 2
F32 = jnp.float32
BF16 = jnp.bfloat16
MESH = pl.DeviceIdType.MESH
VMEM_LIMIT = 60 * 1024 * 1024


def halves(x):
    high = x.astype(BF16)
    return high, (x - high.astype(F32)).astype(BF16)


def host_halves(table):
    table = table.astype(np.float32)
    high = table.astype(BF16)
    low = (table - high.astype(np.float32)).astype(BF16)
    return np.stack([high, low])


def dot3(a, b, dims=((1,), (0,))):
    product = functools.partial(
        lax.dot_general, dimension_numbers=(dims, ((), ())), preferred_element_type=F32
    )
    return product(a[0], b[0]) + (product(a[0], b[1]) + product(a[1], b[0]))


def circle(rows, columns, length):
    angle = (np.outer(rows, columns) % length) * (2.0 * np.pi / length)
    return np.cos(angle), np.sin(angle)


def x_table(parity, width):
    half = width // 2
    cosine, sine = circle(2 * np.arange(half // 2) + parity, np.arange(half), width)
    sine = -sine
    if parity == 0:
        sine[0] = 1.0 - 2.0 * (np.arange(half) % 2)
    return np.stack([cosine, sine], axis=1)


def reduce_forward(
    shots, slabs, sign_ref, size_ref, factor_ref, source_ref, recv_ref, model_ref, tx_ref, column_ref, g_ref, levels,
    acc, along_x, power_ref, shares, source_buf, recv_buf, model_buf, in_sem, chain_send, chain_recv,
    ex_send, ex_recv, own_sem, share_send, share_recv,
):
    shot = lax.axis_index("shot")
    slab = lax.axis_index("slab")
    local, height, width = source_ref.shape
    planes = model_ref.shape[0]
    half = width // 2
    pieces = height // LANES
    parts = height // ROWS
    chunks = local * parts
    groups = g_ref.shape[0]
    rows = along_x.shape[4]
    hops = (shots - 1 - shot, shot)
    last = shots - 1
    parity = jnp.where(shot == 0, 0, 1)
    me = parity * slabs + slab
    wedges = size_ref.shape[0]
    base = chunks * (1 + 4 * (LAG * shots + AHEAD) // chunks)

    def inputs(way, chunk):
        slot = lax.rem(chunk, BUFFERS)
        plane = chunk // parts
        span = pl.ds(pl.multiple_of(lax.rem(chunk, parts) * ROWS, ROWS), ROWS)
        return (
            pltpu.make_async_copy(
                source_ref.at[plane, span], source_buf.at[way, slot], in_sem.at[way, slot, 0]
            ),
            pltpu.make_async_copy(
                recv_ref.at[:, plane, span], recv_buf.at[way, slot], in_sem.at[way, slot, 1]
            ),
        )

    def own_model(way, chunk):
        slot = lax.rem(chunk, BUFFERS)
        plane = chunk // parts
        span = pl.ds(pl.multiple_of(lax.rem(chunk, parts) * ROWS, ROWS), ROWS)
        return pltpu.make_async_copy(
            model_ref.at[lax.rem(plane, planes), span], model_buf.at[way, slot], in_sem.at[way, slot, 2]
        )

    def owned(chunk):
        return chunk // parts // planes == shot

    def exchange(plane, piece, other):
        return pltpu.make_async_remote_copy(
            src_ref=along_x.at[plane, other, :, piece],
            dst_ref=g_ref.at[:, piece, pl.ds(pl.multiple_of((slab * local + plane) * rows, rows), rows)],
            send_sem=ex_send.at[other],
            recv_sem=ex_recv.at[slab],
            device_id=(shot, other),
            device_id_type=MESH,
        )

    def keep(plane, piece):
        return pltpu.make_async_copy(
            along_x.at[plane, slab, :, piece],
            g_ref.at[:, piece, pl.ds(pl.multiple_of((slab * local + plane) * rows, rows), rows)],
            own_sem,
        )

    def join(way, low, high):
        return low + high if way == 0 else low - high

    def share(source, to):
        return pltpu.make_async_remote_copy(
            src_ref=shares.at[source],
            dst_ref=shares.at[source],
            send_sem=share_send.at[to],
            recv_sem=share_recv.at[source],
            device_id=(to // slabs * last, lax.rem(to, slabs)),
            device_id_type=MESH,
        )

    def wedge_vectors():
        lane = lax.broadcasted_iota(jnp.int32, (1, LANES), 1)
        starts = jnp.zeros((1, LANES), jnp.int32)
        sizes = jnp.zeros((1, LANES), jnp.int32)
        factors = jnp.zeros((1, LANES), F32)
        start = 0
        for wedge in range(wedges):
            starts = jnp.where(lane == wedge, start, starts)
            sizes = jnp.where(lane == wedge, size_ref[wedge], sizes)
            factors = jnp.where(lane == wedge, factor_ref[wedge], factors)
            start = start + size_ref[wedge]
        return starts, sizes, factors

    def members_of(columns, starts, sizes):
        return jnp.where((columns >= starts) & (columns < starts + sizes), 1.0, 0.0)

    def mirrored(columns):
        return jnp.where(columns == 0, 0, width - columns)

    def offer_power():
        starts, sizes, _ = wedge_vectors()
        columns = column_ref[parity]
        paired = mirrored(columns)
        counted = members_of(columns, starts, sizes)
        counted = counted + jnp.where(paired == columns, 0.0, members_of(paired, starts, sizes))
        summed = jnp.sum(power_ref[...], axis=1, keepdims=True)
        own = jnp.sum(counted * summed, axis=0, keepdims=True)
        shares[me] = jnp.broadcast_to(own, shares.shape[1:])

        def give(offset, carry):
            share(me, lax.rem(me + offset, 2 * slabs)).start()
            return carry

        lax.fori_loop(1, 2 * slabs, give, 0)

    def take_levels():
        def take(offset, carry):
            other = lax.rem(me + offset, 2 * slabs)
            pltpu.make_async_copy(shares.at[other], shares.at[other], share_send.at[other]).wait()
            pltpu.make_async_copy(shares.at[other], shares.at[other], share_recv.at[other]).wait()
            return carry

        lax.fori_loop(1, 2 * slabs, take, 0)
        starts, sizes, factors = wedge_vectors()
        total = jnp.sum(shares[...], axis=0)[:1]
        heights = factors * jnp.sqrt(total / jnp.maximum(sizes, 1).astype(F32) + EPSILON)
        index = lax.broadcasted_iota(jnp.int32, (levels.shape[1], LANES), 0)
        columns = jnp.where(index == groups * (rows // 2), width // 2, 2 * (slab * groups * (rows // 2) + index) + parity)
        for side, picked in enumerate((columns, mirrored(columns))):
            level = jnp.sum(members_of(picked, starts, sizes) * heights, axis=1, keepdims=True)
            levels[side] = jnp.broadcast_to(level, levels.shape[1:])

    power_ref[...] = jnp.zeros_like(power_ref)
    levels[...] = jnp.zeros_like(levels)

    def fetch(t):
        for way in range(2):
            count = t + base - LAG * hops[way]
            chunk = lax.rem(count, chunks)

            @pl.when((count >= base) & (count < base + chunks))
            def _():
                for copy in inputs(way, chunk):
                    copy.start()

                @pl.when(owned(chunk))
                def _():
                    own_model(way, chunk).start()

    def step(t, carry):
        fetch(t)
        for way in range(2):
            count = t - AHEAD + base - LAG * hops[way]
            chunk = lax.rem(count, chunks)

            @pl.when((count >= base) & (count < base + chunks))
            def _():
                slot = lax.rem(chunk, BUFFERS)
                rows_here = pl.ds(pl.multiple_of(chunk * ROWS, ROWS), ROWS)
                here = acc.at[way, rows_here]
                for copy in inputs(way, chunk):
                    copy.wait()
                encoded = jnp.zeros((ROWS, width), F32)
                for member in range(recv_ref.shape[0]):
                    encoded = encoded + sign_ref[member].astype(F32) * recv_buf[way, slot, member].astype(F32)
                part = -STEP_SIZE * (source_buf[way, slot].astype(F32) * encoded)
                part = join(way, part[:, :half], part[:, half:])

                @pl.when(hops[way] > 0)
                def _():
                    pltpu.make_async_copy(here, here, chain_recv.at[way, chunk]).wait()
                    acc[way, rows_here] = acc[way, rows_here] + part

                @pl.when(hops[way] == 0)
                def _():
                    acc[way, rows_here] = part

                @pl.when(owned(chunk))
                def _():
                    own_model(way, chunk).wait()
                    image = model_buf[way, slot].astype(F32)
                    acc[way, rows_here] = acc[way, rows_here] + join(way, image[:, :half], image[:, half:])

                @pl.when(hops[way] < last)
                def _():
                    pltpu.make_async_remote_copy(
                        src_ref=here,
                        dst_ref=here,
                        send_sem=chain_send.at[way],
                        recv_sem=chain_recv.at[way, chunk],
                        device_id=(shot - 1 + 2 * way, slab),
                        device_id_type=MESH,
                    ).start()

                per_piece = LANES // ROWS

                @pl.when((hops[way] == last) & (lax.rem(chunk, per_piece) == per_piece - 1))
                def _():
                    plane = chunk // parts
                    first = chunk // per_piece
                    piece = lax.rem(first, pieces)
                    summed = acc[way, pl.ds(pl.multiple_of(first * LANES, LANES), LANES)]
                    result = dot3((tx_ref[way, 0], tx_ref[way, 1]), halves(summed), ((1,), (1,)))
                    power_ref[...] = power_ref[...] + result * result
                    along_x[plane, :, :, piece] = result.reshape(slabs, groups, rows, LANES)

                    def send(offset, carry):
                        exchange(plane, piece, lax.rem(slab + offset, slabs)).start()
                        return carry

                    lax.fori_loop(1, slabs, send, 0)
                    keep(plane, piece).start()

        return carry

    end = (shot == 0) | (shot == last)
    barrier = pltpu.get_barrier_semaphore()

    def greet(to_shot, to_slab):
        pl.semaphore_signal(barrier, inc=1, device_id=(to_shot, to_slab), device_id_type=MESH)

    @pl.when(shot > 0)
    def _():
        greet(shot - 1, slab)

    @pl.when(shot < last)
    def _():
        greet(shot + 1, slab)

    @pl.when(end)
    def _():
        def greet_end(offset, carry):
            other = lax.rem(me + offset, 2 * slabs)
            greet(other // slabs * last, lax.rem(other, slabs))
            return carry

        lax.fori_loop(1, 2 * slabs, greet_end, 0)

    for t in range(AHEAD):
        fetch(t)

    @pl.when(end)
    def _():
        pl.semaphore_wait(barrier, 2 * slabs)

    @pl.when(jnp.logical_not(end))
    def _():
        pl.semaphore_wait(barrier, 2)

    lax.fori_loop(AHEAD, chunks + LAG * last + AHEAD, step, 0)

    pl.when(end)(offer_power)

    for way in range(2):

        @pl.when(hops[way] < last)
        def _():
            sent = acc.at[way]
            pltpu.make_async_copy(sent, sent, chain_send.at[way]).wait()

    @pl.when(end)
    def _():
        def part_of(other):
            return g_ref.at[:, :, pl.ds(pl.multiple_of(other * local * rows, rows), local * rows)]

        def finish(offset, carry):
            other = lax.rem(slab + offset, slabs)
            piece = part_of(other)
            pltpu.make_async_copy(piece, piece, ex_send.at[other]).wait()
            pltpu.make_async_copy(piece, piece, ex_recv.at[other]).wait()
            return carry

        lax.fori_loop(1, slabs, finish, 0)
        mine = part_of(slab)
        pltpu.make_async_copy(mine, mine, own_sem).wait()
        take_levels()


def shrink_back(
    shots, slabs, x_width, level_ref, tz_ref, ty_ref, g_ref, r_ref, held, out, send_sem, recv_sem, own_sem
):
    step = pl.program_id(0)
    slot = pl.num_programs(0) - 1 - step
    shot = lax.axis_index("shot")
    slab = lax.axis_index("slab")
    slots, _, pieces, depth, _ = out.shape
    width = pieces * LANES
    planes = r_ref.shape[4]
    rows = g_ref.shape[1] // depth
    devices = shots * slabs
    last = shots - 1
    end = (shot == 0) | (shot == last)
    me = jnp.where(shot == 0, 0, slabs) + slab

    def along_y(re, im, sign):
        result = dot3(halves(jnp.concatenate([re, im], axis=0)), (ty_ref[0], ty_ref[1]))
        with_cos, with_sin = result[:, :width], result[:, width:]
        return (
            with_cos[:depth] + sign * with_sin[depth:],
            with_cos[depth:] - sign * with_sin[:depth],
        )

    def along_z(re, im, sign):
        result = dot3((tz_ref[0], tz_ref[1]), halves(jnp.concatenate([re, im], axis=1)))
        with_cos, with_sin = result[:depth], result[depth:]
        return (
            with_cos[:, :width] + sign * with_sin[:, width:],
            with_cos[:, width:] - sign * with_sin[:, :width],
        )

    def target(index):
        far = index // slabs
        to_shot = jnp.where(shot == 0, last - far, far)
        to_slab = lax.rem(slab + index, slabs)
        return to_shot, to_slab

    def part(to_shot, to_slab):
        first = to_slab * (shots * planes) + to_shot * planes
        return out.at[slot, :, :, pl.ds(pl.multiple_of(first, planes), planes)]

    barrier = pltpu.get_barrier_semaphore()

    @pl.when(step == 0)
    def _():
        def greet(index, carry):
            to_shot, to_slab = target(index)
            met = end | (to_shot == 0) | (to_shot == last)

            @pl.when(met & ((to_shot != shot) | (to_slab != slab)))
            def _():
                pl.semaphore_signal(barrier, inc=1, device_id=(to_shot, to_slab), device_id_type=MESH)

            return carry

        lax.fori_loop(0, devices, greet, 0)

    @pl.when(end)
    def _():
        packed = (shot == 0) & (slab == 0) & (slot == 0)
        row = lax.rem(slot, rows // 2)

        def spread(first):
            return jnp.concatenate(
                [g_ref[piece, pl.ds(first, depth, stride=rows), :] for piece in range(pieces)], axis=1
            )

        def column(which, carry):
            re = spread(row + which * (rows // 2))
            im = jnp.where(packed, 0.0, spread(row + rows // 2))
            re, im = along_z(*along_y(re, im, 1.0), 1.0)

            index = slot + which * slots
            magnitude = jnp.sqrt(re * re + im * im)
            total = 0.0
            for side in range(2):
                level = level_ref[side, pl.ds(index, 1)]
                total = total + jnp.maximum(magnitude - level, 0.0) / jnp.maximum(magnitude, level)
            total = total * (jnp.where(packed, 0.5, 1.0) * (1.0 / (depth * width * x_width)))
            re, im = re * total, im * total

            @pl.when(which == 0)
            def _():
                held[0] = re
                held[1] = im

            @pl.when(which == 1)
            def _():
                held[0] = held[0] - im
                held[1] = held[1] + re

            return carry

        lax.fori_loop(0, jnp.where(packed, 2, 1), column, 0)
        re, im = along_y(*along_z(held[0], held[1], -1.0), -1.0)
        for piece in range(pieces):
            span = slice(piece * LANES, (piece + 1) * LANES)
            out[slot, 0, piece] = re[:, span]
            out[slot, 1, piece] = im[:, span]

    @pl.when((step == 0) & end)
    def _():
        pl.semaphore_wait(barrier, devices - 1)

    @pl.when((step == 0) & jnp.logical_not(end))
    def _():
        pl.semaphore_wait(barrier, 2 * slabs)

    @pl.when(end)
    def _():
        def send(index, carry):
            to_shot, to_slab = target(index)

            @pl.when((to_shot != shot) | (to_slab != slab))
            def _():
                pltpu.make_async_remote_copy(
                    src_ref=part(to_shot, to_slab),
                    dst_ref=r_ref.at[me, slot],
                    send_sem=send_sem.at[to_shot, to_slab],
                    recv_sem=recv_sem.at[me],
                    device_id=(to_shot, to_slab),
                    device_id_type=MESH,
                ).start()

            return carry

        lax.fori_loop(0, devices, send, 0)
        pltpu.make_async_copy(part(shot, slab), r_ref.at[me, slot], own_sem).start()

    @pl.when(step == slots - 1)
    def _():
        @pl.when(end)
        def _():
            def sent(index, carry):
                to_shot, to_slab = target(index)

                @pl.when((to_shot != shot) | (to_slab != slab))
                def _():
                    pltpu.make_async_copy(r_ref.at[0], r_ref.at[0], send_sem.at[to_shot, to_slab]).wait()

                return carry

            lax.fori_loop(0, devices, sent, 0)
            pltpu.make_async_copy(r_ref.at[me], r_ref.at[me], own_sem).wait()

        def arrived(index, carry):
            @pl.when(jnp.logical_not(end) | (index != me))
            def _():
                pltpu.make_async_copy(r_ref.at[index], r_ref.at[index], recv_sem.at[index]).wait()

            return carry

        lax.fori_loop(0, 2 * slabs, arrived, 0)


def inverse_x(planes, pieces, r_ref, tx_ref, out_ref):
    count = tx_ref.shape[2]
    pitch = pieces * planes
    batch = out_ref.shape[0]

    def side(parity):
        terms = jnp.concatenate(
            [
                r_ref[
                    pl.ds(
                        parity * count * pitch + piece * planes + pl.program_id(0) * batch + plane,
                        count,
                        stride=pitch,
                    ),
                    :,
                ]
                for plane in range(batch)
                for piece in range(pieces)
            ],
            axis=1,
        )
        return dot3(halves(terms), (tx_ref[parity, 0], tx_ref[parity, 1]), ((0,), (0,)))

    even, odd = side(0), side(1)
    half = even.shape[1]
    out_ref[:, :, :half] = (even + odd).reshape(batch, -1, half)
    out_ref[:, :, half:] = (even - odd).reshape(batch, -1, half)


def whole_block(array, memory_space=None):
    if memory_space is not None:
        return pl.BlockSpec(memory_space=memory_space)
    zeros = (0,) * array.ndim
    return pl.BlockSpec(array.shape, lambda *_: zeros)


def on_device(source_field, receiver_fields, weights, model, wedge_sizes, wedge_scales):
    shots = lax.axis_size("shot")
    slabs = lax.axis_size("slab")
    shot = lax.axis_index("shot")
    slab = lax.axis_index("slab")
    devices = shots * slabs
    members, local, height, width = receiver_fields.shape
    planes = model.shape[0]
    depth = local * slabs
    half = width // 2
    slots = half // 2 // slabs
    four = min(4, slots)
    groups, rows = slots // four, 2 * four
    pieces = height // LANES
    chunks = local * (height // ROWS)
    params = functools.partial(pltpu.CompilerParams, vmem_limit_bytes=VMEM_LIMIT)

    tables = [x_table(parity, width).reshape(slabs, groups, four, 2, half) for parity in range(2)]
    tx = np.stack([host_halves(t.transpose(0, 1, 3, 2, 4).reshape(half, half)) for t in tables])
    tx_back = np.stack([host_halves(t.reshape(half, half)) for t in tables])
    ty = host_halves(np.concatenate(circle(np.arange(height), np.arange(height), height), axis=1))
    tz = host_halves(np.concatenate(circle(np.arange(depth), np.arange(depth), depth), axis=0))
    tx, tx_back, ty, tz = (jnp.asarray(table) for table in (tx, tx_back, ty, tz))

    row_slots = (
        np.arange(slabs)[:, None, None, None] * slots
        + np.arange(groups)[:, None, None] * four
        + np.zeros((2, 1), np.int32)
        + np.arange(four)
    ).reshape(-1)
    row_columns = 2 * row_slots + np.arange(2)[:, None]
    row_columns[0, four] = half
    row_columns = np.broadcast_to(row_columns[:, :, None], (2, half, LANES)).astype(np.int32)
    row_columns = jnp.asarray(row_columns)

    anywhere = pl.BlockSpec(memory_space=pl.ANY)
    gathered, levels = pl.pallas_call(
        functools.partial(reduce_forward, shots, slabs),
        out_shape=(
            jax.ShapeDtypeStruct((groups, pieces, depth * rows, LANES), F32),
            jax.ShapeDtypeStruct((2, slots // 8 * 8 + 8, height), F32),
        ),
        in_specs=[
            pl.BlockSpec(memory_space=pltpu.SMEM),
            pl.BlockSpec(memory_space=pltpu.SMEM),
            pl.BlockSpec(memory_space=pltpu.SMEM),
            anywhere,
            anywhere,
            anywhere,
            pl.BlockSpec(memory_space=pltpu.VMEM),
            pl.BlockSpec(memory_space=pltpu.VMEM),
        ],
        out_specs=(anywhere, pl.BlockSpec(memory_space=pltpu.VMEM)),
        scratch_shapes=[
            pltpu.VMEM((2, local * height, half), F32),
            pltpu.VMEM((local, slabs, groups, pieces, rows, LANES), F32),
            pltpu.VMEM((half, LANES), F32),
            pltpu.VMEM((2 * slabs, 8, LANES), F32),
            pltpu.VMEM((2, BUFFERS, ROWS, width), BF16),
            pltpu.VMEM((2, BUFFERS, members, ROWS, width), BF16),
            pltpu.VMEM((2, BUFFERS, ROWS, width), BF16),
            pltpu.SemaphoreType.DMA((2, BUFFERS, 3)),
            pltpu.SemaphoreType.DMA((2,)),
            pltpu.SemaphoreType.DMA((2, chunks)),
            pltpu.SemaphoreType.DMA((slabs,)),
            pltpu.SemaphoreType.DMA((slabs,)),
            pltpu.SemaphoreType.DMA,
            pltpu.SemaphoreType.DMA((2 * slabs,)),
            pltpu.SemaphoreType.DMA((2 * slabs,)),
        ],
        compiler_params=params(collective_id=0, has_side_effects=True),
    )(weights, wedge_sizes, wedge_scales, source_field[0], receiver_fields, model, tx, row_columns)

    returned = pl.pallas_call(
        functools.partial(shrink_back, shots, slabs, width),
        out_shape=jax.ShapeDtypeStruct((2 * slabs, slots, 2, pieces, planes, LANES), F32),
        grid=(slots,),
        in_specs=[
            whole_block(levels),
            whole_block(tz),
            whole_block(ty),
            pl.BlockSpec((None, pieces, depth * rows, LANES), lambda k: ((slots - 1 - k) // four, 0, 0, 0)),
        ],
        out_specs=anywhere,
        scratch_shapes=[
            pltpu.VMEM((2, depth, height), F32),
            pltpu.VMEM((slots, 2, pieces, depth, LANES), F32),
            pltpu.SemaphoreType.DMA((shots, slabs)),
            pltpu.SemaphoreType.DMA((2 * slabs,)),
            pltpu.SemaphoreType.DMA,
        ],
        compiler_params=params(collective_id=1, has_side_effects=True),
    )(levels, tz, ty, gathered)

    batch = math.gcd(planes, 2)
    terms = returned.reshape(2 * half * pieces * planes, LANES)
    return pl.pallas_call(
        functools.partial(inverse_x, planes, pieces),
        out_shape=jax.ShapeDtypeStruct((planes, height, width), F32),
        grid=(planes // batch,),
        in_specs=[whole_block(terms), whole_block(tx_back)],
        out_specs=pl.BlockSpec((batch, height, width), lambda z: (z, 0, 0)),
        compiler_params=params(),
    )(terms, tx_back)


def solution(mesh):
    placed = (
        P("shot", "slab", None, None),
        P("shot", "slab", None, None),
        P("shot"),
        P(("slab", "shot"), None, None),
        P(),
        P(),
    )
    return jax.shard_map(
        on_device,
        mesh=mesh,
        in_specs=placed,
        out_specs=P(("slab", "shot"), None, None),
        check_vma=False,
    )
```

```python
import functools
import math

import jax
import jax.numpy as jnp
import numpy as np
from jax import lax
from jax.experimental import pallas as pl
from jax.experimental.pallas import tpu as pltpu
from jax.sharding import PartitionSpec as P

STEP_SIZE = 0.25
EPSILON = 1e-06
LANES = 128
ROWS = 64
LAG = 3
BUFFERS = 4
AHEAD = 2
F32 = jnp.float32
BF16 = jnp.bfloat16
MESH = pl.DeviceIdType.MESH
VMEM_LIMIT = 60 * 1024 * 1024


def halves(x):
    high = x.astype(BF16)
    return high, (x - high.astype(F32)).astype(BF16)


def host_halves(table):
    table = table.astype(np.float32)
    high = table.astype(BF16)
    low = (table - high.astype(np.float32)).astype(BF16)
    return np.stack([high, low])


def dot3(a, b, dims=((1,), (0,))):
    product = functools.partial(
        lax.dot_general, dimension_numbers=(dims, ((), ())), preferred_element_type=F32
    )
    return product(a[0], b[0]) + (product(a[0], b[1]) + product(a[1], b[0]))


def circle(rows, columns, length):
    angle = (np.outer(rows, columns) % length) * (2.0 * np.pi / length)
    return np.cos(angle), np.sin(angle)


def x_table(parity, width):
    half = width // 2
    cosine, sine = circle(2 * np.arange(half // 2) + parity, np.arange(half), width)
    sine = -sine
    if parity == 0:
        sine[0] = 1.0 - 2.0 * (np.arange(half) % 2)
    return np.stack([cosine, sine], axis=1)


def reduce_forward(
    shots, slabs, sign_ref, size_ref, factor_ref, source_ref, recv_ref, model_ref, tx_any, column_any,
    g_ref, levels,
    acc, along_x, power_ref, shares, source_buf, recv_buf, model_buf, in_sem, chain_send, chain_recv,
    ex_send, ex_recv, own_sem, share_send, share_recv, tx_ref, column_ref, counted_ref, table_sem,
):
    shot = lax.axis_index("shot")
    slab = lax.axis_index("slab")
    local, height, width = source_ref.shape
    planes = model_ref.shape[0]
    half = width // 2
    pieces = height // LANES
    parts = height // ROWS
    chunks = local * parts
    groups = g_ref.shape[0]
    rows = along_x.shape[4]
    hops = (shots - 1 - shot, shot)
    last = shots - 1
    parity = jnp.where(shot == 0, 0, 1)
    me = parity * slabs + slab
    wedges = size_ref.shape[0]
    base = chunks * (1 + 4 * (LAG * shots + AHEAD) // chunks)

    def inputs(way, chunk):
        slot = lax.rem(chunk, BUFFERS)
        plane = chunk // parts
        span = pl.ds(pl.multiple_of(lax.rem(chunk, parts) * ROWS, ROWS), ROWS)
        return (
            pltpu.make_async_copy(
                source_ref.at[plane, span], source_buf.at[way, slot], in_sem.at[way, slot, 0]
            ),
            pltpu.make_async_copy(
                recv_ref.at[:, plane, span], recv_buf.at[way, slot], in_sem.at[way, slot, 1]
            ),
        )

    def own_model(way, chunk):
        slot = lax.rem(chunk, BUFFERS)
        plane = chunk // parts
        span = pl.ds(pl.multiple_of(lax.rem(chunk, parts) * ROWS, ROWS), ROWS)
        return pltpu.make_async_copy(
            model_ref.at[lax.rem(plane, planes), span], model_buf.at[way, slot], in_sem.at[way, slot, 2]
        )

    def owned(chunk):
        return chunk // parts // planes == shot

    def exchange(plane, piece, other):
        return pltpu.make_async_remote_copy(
            src_ref=along_x.at[plane, other, :, piece],
            dst_ref=g_ref.at[:, piece, pl.ds(pl.multiple_of((slab * local + plane) * rows, rows), rows)],
            send_sem=ex_send.at[other],
            recv_sem=ex_recv.at[slab],
            device_id=(shot, other),
            device_id_type=MESH,
        )

    def keep(plane, piece):
        return pltpu.make_async_copy(
            along_x.at[plane, slab, :, piece],
            g_ref.at[:, piece, pl.ds(pl.multiple_of((slab * local + plane) * rows, rows), rows)],
            own_sem,
        )

    def join(way, low, high):
        return low + high if way == 0 else low - high

    def share(source, to):
        return pltpu.make_async_remote_copy(
            src_ref=shares.at[source],
            dst_ref=shares.at[source],
            send_sem=share_send.at[to],
            recv_sem=share_recv.at[source],
            device_id=(to // slabs * last, lax.rem(to, slabs)),
            device_id_type=MESH,
        )

    def wedge_vectors():
        lane = lax.broadcasted_iota(jnp.int32, (1, LANES), 1)
        starts = jnp.zeros((1, LANES), jnp.int32)
        sizes = jnp.zeros((1, LANES), jnp.int32)
        factors = jnp.zeros((1, LANES), F32)
        start = 0
        for wedge in range(wedges):
            starts = jnp.where(lane == wedge, start, starts)
            sizes = jnp.where(lane == wedge, size_ref[wedge], sizes)
            factors = jnp.where(lane == wedge, factor_ref[wedge], factors)
            start = start + size_ref[wedge]
        return starts, sizes, factors

    def members_of(columns, starts, sizes):
        return jnp.where((columns >= starts) & (columns < starts + sizes), 1.0, 0.0)

    def mirrored(columns):
        return jnp.where(columns == 0, 0, width - columns)

    def count_members():
        starts, sizes, _ = wedge_vectors()
        columns = column_ref[...]
        paired = mirrored(columns)
        counted = members_of(columns, starts, sizes)
        counted_ref[...] = counted + jnp.where(paired == columns, 0.0, members_of(paired, starts, sizes))

    def offer_power():
        summed = jnp.sum(power_ref[...], axis=1, keepdims=True)
        own = jnp.sum(counted_ref[...] * summed, axis=0, keepdims=True)
        shares[me] = jnp.broadcast_to(own, shares.shape[1:])

        def give(offset, carry):
            share(me, lax.rem(me + offset, 2 * slabs)).start()
            return carry

        lax.fori_loop(1, 2 * slabs, give, 0)

    def take_levels():
        def take(offset, carry):
            other = lax.rem(me + offset, 2 * slabs)
            pltpu.make_async_copy(shares.at[other], shares.at[other], share_send.at[other]).wait()
            pltpu.make_async_copy(shares.at[other], shares.at[other], share_recv.at[other]).wait()
            return carry

        lax.fori_loop(1, 2 * slabs, take, 0)
        starts, sizes, factors = wedge_vectors()
        total = jnp.sum(shares[...], axis=0)[:1]
        heights = factors * jnp.sqrt(total / jnp.maximum(sizes, 1).astype(F32) + EPSILON)
        index = lax.broadcasted_iota(jnp.int32, (levels.shape[1], LANES), 0)
        columns = jnp.where(index == groups * (rows // 2), width // 2, 2 * (slab * groups * (rows // 2) + index) + parity)
        for side, picked in enumerate((columns, mirrored(columns))):
            level = jnp.sum(members_of(picked, starts, sizes) * heights, axis=1, keepdims=True)
            levels[side] = jnp.broadcast_to(level, levels.shape[1:])

    end = (shot == 0) | (shot == last)
    power_ref[...] = jnp.zeros_like(power_ref)
    levels[...] = jnp.zeros_like(levels)

    def fetch(t):
        for way in range(2):
            count = t + base - LAG * hops[way]
            chunk = lax.rem(count, chunks)

            @pl.when((count >= base) & (count < base + chunks))
            def _():
                for copy in inputs(way, chunk):
                    copy.start()

                @pl.when(owned(chunk))
                def _():
                    own_model(way, chunk).start()

    def step(t, carry):
        fetch(t)
        pl.when(end & (t == AHEAD + LAG * last))(count_members)
        for way in range(2):
            count = t - AHEAD + base - LAG * hops[way]
            chunk = lax.rem(count, chunks)

            @pl.when((count >= base) & (count < base + chunks))
            def _():
                slot = lax.rem(chunk, BUFFERS)
                rows_here = pl.ds(pl.multiple_of(chunk * ROWS, ROWS), ROWS)
                here = acc.at[way, rows_here]
                for copy in inputs(way, chunk):
                    copy.wait()
                encoded = jnp.zeros((ROWS, width), F32)
                for member in range(recv_ref.shape[0]):
                    encoded = encoded + sign_ref[member].astype(F32) * recv_buf[way, slot, member].astype(F32)
                part = -STEP_SIZE * (source_buf[way, slot].astype(F32) * encoded)
                part = join(way, part[:, :half], part[:, half:])

                @pl.when(hops[way] > 0)
                def _():
                    pltpu.make_async_copy(here, here, chain_recv.at[way, chunk]).wait()
                    acc[way, rows_here] = acc[way, rows_here] + part

                @pl.when(hops[way] == 0)
                def _():
                    acc[way, rows_here] = part

                @pl.when(owned(chunk))
                def _():
                    own_model(way, chunk).wait()
                    image = model_buf[way, slot].astype(F32)
                    acc[way, rows_here] = acc[way, rows_here] + join(way, image[:, :half], image[:, half:])

                @pl.when(hops[way] < last)
                def _():
                    pltpu.make_async_remote_copy(
                        src_ref=here,
                        dst_ref=here,
                        send_sem=chain_send.at[way],
                        recv_sem=chain_recv.at[way, chunk],
                        device_id=(shot - 1 + 2 * way, slab),
                        device_id_type=MESH,
                    ).start()

                per_piece = LANES // ROWS

                @pl.when((hops[way] == last) & (lax.rem(chunk, per_piece) == per_piece - 1))
                def _():
                    plane = chunk // parts
                    first = chunk // per_piece
                    piece = lax.rem(first, pieces)
                    summed = acc[way, pl.ds(pl.multiple_of(first * LANES, LANES), LANES)]
                    result = dot3((tx_ref[way, 0], tx_ref[way, 1]), halves(summed), ((1,), (1,)))
                    power_ref[...] = power_ref[...] + result * result
                    along_x[plane, :, :, piece] = result.reshape(slabs, groups, rows, LANES)

                    def send(offset, carry):
                        exchange(plane, piece, lax.rem(slab + offset, slabs)).start()
                        return carry

                    lax.fori_loop(1, slabs, send, 0)
                    keep(plane, piece).start()

        return carry

    barrier = pltpu.get_barrier_semaphore()

    def greet(to_shot, to_slab):
        pl.semaphore_signal(barrier, inc=1, device_id=(to_shot, to_slab), device_id_type=MESH)

    @pl.when(shot > 0)
    def _():
        greet(shot - 1, slab)

    @pl.when(shot < last)
    def _():
        greet(shot + 1, slab)

    @pl.when(end)
    def _():
        def greet_end(offset, carry):
            other = lax.rem(me + offset, 2 * slabs)
            greet(other // slabs * last, lax.rem(other, slabs))
            return carry

        lax.fori_loop(1, 2 * slabs, greet_end, 0)

    for t in range(AHEAD):
        fetch(t)
    tables = (
        pltpu.make_async_copy(tx_any, tx_ref, table_sem.at[0]),
        pltpu.make_async_copy(column_any.at[parity], column_ref, table_sem.at[1]),
    )
    for copy in tables:
        copy.start()

    @pl.when(end)
    def _():
        pl.semaphore_wait(barrier, 2 * slabs)

    @pl.when(jnp.logical_not(end))
    def _():
        pl.semaphore_wait(barrier, 2)

    for copy in tables:
        copy.wait()
    lax.fori_loop(AHEAD, chunks + LAG * last + AHEAD, step, 0)

    pl.when(end)(offer_power)

    for way in range(2):

        @pl.when(hops[way] < last)
        def _():
            sent = acc.at[way]
            pltpu.make_async_copy(sent, sent, chain_send.at[way]).wait()

    @pl.when(end)
    def _():
        def part_of(other):
            return g_ref.at[:, :, pl.ds(pl.multiple_of(other * local * rows, rows), local * rows)]

        def finish(offset, carry):
            other = lax.rem(slab + offset, slabs)
            piece = part_of(other)
            pltpu.make_async_copy(piece, piece, ex_send.at[other]).wait()
            pltpu.make_async_copy(piece, piece, ex_recv.at[other]).wait()
            return carry

        lax.fori_loop(1, slabs, finish, 0)
        mine = part_of(slab)
        pltpu.make_async_copy(mine, mine, own_sem).wait()
        take_levels()


def shrink_back(
    shots, slabs, x_width, level_ref, tz_ref, ty_ref, g_ref, r_ref, held, out, send_sem, recv_sem, own_sem
):
    step = pl.program_id(0)
    slot = pl.num_programs(0) - 1 - step
    shot = lax.axis_index("shot")
    slab = lax.axis_index("slab")
    slots, _, pieces, depth, _ = out.shape
    width = pieces * LANES
    planes = r_ref.shape[4]
    rows = g_ref.shape[1] // depth
    devices = shots * slabs
    last = shots - 1
    end = (shot == 0) | (shot == last)
    me = jnp.where(shot == 0, 0, slabs) + slab

    def along_y(re, im, sign):
        result = dot3(halves(jnp.concatenate([re, im], axis=0)), (ty_ref[0], ty_ref[1]))
        with_cos, with_sin = result[:, :width], result[:, width:]
        return (
            with_cos[:depth] + sign * with_sin[depth:],
            with_cos[depth:] - sign * with_sin[:depth],
        )

    def along_z(re, im, sign):
        result = dot3((tz_ref[0], tz_ref[1]), halves(jnp.concatenate([re, im], axis=1)))
        with_cos, with_sin = result[:depth], result[depth:]
        return (
            with_cos[:, :width] + sign * with_sin[:, width:],
            with_cos[:, width:] - sign * with_sin[:, :width],
        )

    def target(index):
        far = index // slabs
        to_shot = jnp.where(shot == 0, last - far, far)
        to_slab = lax.rem(slab + index, slabs)
        return to_shot, to_slab

    def part(to_shot, to_slab):
        first = to_slab * (shots * planes) + to_shot * planes
        return out.at[slot, :, :, pl.ds(pl.multiple_of(first, planes), planes)]

    barrier = pltpu.get_barrier_semaphore()

    @pl.when(step == 0)
    def _():
        def greet(index, carry):
            to_shot, to_slab = target(index)
            met = end | (to_shot == 0) | (to_shot == last)

            @pl.when(met & ((to_shot != shot) | (to_slab != slab)))
            def _():
                pl.semaphore_signal(barrier, inc=1, device_id=(to_shot, to_slab), device_id_type=MESH)

            return carry

        lax.fori_loop(0, devices, greet, 0)

    @pl.when(end)
    def _():
        packed = (shot == 0) & (slab == 0) & (slot == 0)
        row = lax.rem(slot, rows // 2)

        def spread(first):
            return jnp.concatenate(
                [g_ref[piece, pl.ds(first, depth, stride=rows), :] for piece in range(pieces)], axis=1
            )

        def column(which, carry):
            re = spread(row + which * (rows // 2))
            im = jnp.where(packed, 0.0, spread(row + rows // 2))
            re, im = along_z(*along_y(re, im, 1.0), 1.0)

            index = slot + which * slots
            magnitude = jnp.sqrt(re * re + im * im)
            total = 0.0
            for side in range(2):
                level = level_ref[side, pl.ds(index, 1)]
                total = total + jnp.maximum(magnitude - level, 0.0) / jnp.maximum(magnitude, level)
            total = total * (jnp.where(packed, 0.5, 1.0) * (1.0 / (depth * width * x_width)))
            re, im = re * total, im * total

            @pl.when(which == 0)
            def _():
                held[0] = re
                held[1] = im

            @pl.when(which == 1)
            def _():
                held[0] = held[0] - im
                held[1] = held[1] + re

            return carry

        lax.fori_loop(0, jnp.where(packed, 2, 1), column, 0)
        re, im = along_y(*along_z(held[0], held[1], -1.0), -1.0)
        for piece in range(pieces):
            span = slice(piece * LANES, (piece + 1) * LANES)
            out[slot, 0, piece] = re[:, span]
            out[slot, 1, piece] = im[:, span]

    @pl.when((step == 0) & end)
    def _():
        pl.semaphore_wait(barrier, devices - 1)

    @pl.when((step == 0) & jnp.logical_not(end))
    def _():
        pl.semaphore_wait(barrier, 2 * slabs)

    @pl.when(end)
    def _():
        def send(index, carry):
            to_shot, to_slab = target(index)

            @pl.when((to_shot != shot) | (to_slab != slab))
            def _():
                pltpu.make_async_remote_copy(
                    src_ref=part(to_shot, to_slab),
                    dst_ref=r_ref.at[me, slot],
                    send_sem=send_sem.at[to_shot, to_slab],
                    recv_sem=recv_sem.at[me],
                    device_id=(to_shot, to_slab),
                    device_id_type=MESH,
                ).start()

            return carry

        lax.fori_loop(0, devices, send, 0)
        pltpu.make_async_copy(part(shot, slab), r_ref.at[me, slot], own_sem).start()

    @pl.when(step == slots - 1)
    def _():
        @pl.when(end)
        def _():
            def sent(index, carry):
                to_shot, to_slab = target(index)

                @pl.when((to_shot != shot) | (to_slab != slab))
                def _():
                    pltpu.make_async_copy(r_ref.at[0], r_ref.at[0], send_sem.at[to_shot, to_slab]).wait()

                return carry

            lax.fori_loop(0, devices, sent, 0)
            pltpu.make_async_copy(r_ref.at[me], r_ref.at[me], own_sem).wait()

        def arrived(index, carry):
            @pl.when(jnp.logical_not(end) | (index != me))
            def _():
                pltpu.make_async_copy(r_ref.at[index], r_ref.at[index], recv_sem.at[index]).wait()

            return carry

        lax.fori_loop(0, 2 * slabs, arrived, 0)


def inverse_x(planes, pieces, r_ref, tx_ref, out_ref):
    count = tx_ref.shape[2]
    pitch = pieces * planes
    batch = out_ref.shape[0]

    def side(parity):
        terms = jnp.concatenate(
            [
                r_ref[
                    pl.ds(
                        parity * count * pitch + piece * planes + pl.program_id(0) * batch + plane,
                        count,
                        stride=pitch,
                    ),
                    :,
                ]
                for plane in range(batch)
                for piece in range(pieces)
            ],
            axis=1,
        )
        return dot3(halves(terms), (tx_ref[parity, 0], tx_ref[parity, 1]), ((0,), (0,)))

    even, odd = side(0), side(1)
    half = even.shape[1]
    out_ref[:, :, :half] = (even + odd).reshape(batch, -1, half)
    out_ref[:, :, half:] = (even - odd).reshape(batch, -1, half)


def whole_block(array, memory_space=None):
    if memory_space is not None:
        return pl.BlockSpec(memory_space=memory_space)
    zeros = (0,) * array.ndim
    return pl.BlockSpec(array.shape, lambda *_: zeros)


def on_device(source_field, receiver_fields, weights, model, wedge_sizes, wedge_scales):
    shots = lax.axis_size("shot")
    slabs = lax.axis_size("slab")
    shot = lax.axis_index("shot")
    slab = lax.axis_index("slab")
    devices = shots * slabs
    members, local, height, width = receiver_fields.shape
    planes = model.shape[0]
    depth = local * slabs
    half = width // 2
    slots = half // 2 // slabs
    four = min(4, slots)
    groups, rows = slots // four, 2 * four
    pieces = height // LANES
    chunks = local * (height // ROWS)
    params = functools.partial(pltpu.CompilerParams, vmem_limit_bytes=VMEM_LIMIT)

    tables = [x_table(parity, width).reshape(slabs, groups, four, 2, half) for parity in range(2)]
    tx = np.stack([host_halves(t.transpose(0, 1, 3, 2, 4).reshape(half, half)) for t in tables])
    tx_back = np.stack([host_halves(t.reshape(half, half)) for t in tables])
    ty = host_halves(np.concatenate(circle(np.arange(height), np.arange(height), height), axis=1))
    tz = host_halves(np.concatenate(circle(np.arange(depth), np.arange(depth), depth), axis=0))
    tx, tx_back, ty, tz = (jnp.asarray(table) for table in (tx, tx_back, ty, tz))

    row_slots = (
        np.arange(slabs)[:, None, None, None] * slots
        + np.arange(groups)[:, None, None] * four
        + np.zeros((2, 1), np.int32)
        + np.arange(four)
    ).reshape(-1)
    row_columns = 2 * row_slots + np.arange(2)[:, None]
    row_columns[0, four] = half
    row_columns = np.broadcast_to(row_columns[:, :, None], (2, half, LANES)).astype(np.int32)
    row_columns = jnp.asarray(row_columns)

    anywhere = pl.BlockSpec(memory_space=pl.ANY)
    gathered, levels = pl.pallas_call(
        functools.partial(reduce_forward, shots, slabs),
        out_shape=(
            jax.ShapeDtypeStruct((groups, pieces, depth * rows, LANES), F32),
            jax.ShapeDtypeStruct((2, slots // 8 * 8 + 8, height), F32),
        ),
        in_specs=[
            pl.BlockSpec(memory_space=pltpu.SMEM),
            pl.BlockSpec(memory_space=pltpu.SMEM),
            pl.BlockSpec(memory_space=pltpu.SMEM),
            anywhere,
            anywhere,
            anywhere,
            anywhere,
            anywhere,
        ],
        out_specs=(anywhere, pl.BlockSpec(memory_space=pltpu.VMEM)),
        scratch_shapes=[
            pltpu.VMEM((2, local * height, half), F32),
            pltpu.VMEM((local, slabs, groups, pieces, rows, LANES), F32),
            pltpu.VMEM((half, LANES), F32),
            pltpu.VMEM((2 * slabs, 8, LANES), F32),
            pltpu.VMEM((2, BUFFERS, ROWS, width), BF16),
            pltpu.VMEM((2, BUFFERS, members, ROWS, width), BF16),
            pltpu.VMEM((2, BUFFERS, ROWS, width), BF16),
            pltpu.SemaphoreType.DMA((2, BUFFERS, 3)),
            pltpu.SemaphoreType.DMA((2,)),
            pltpu.SemaphoreType.DMA((2, chunks)),
            pltpu.SemaphoreType.DMA((slabs,)),
            pltpu.SemaphoreType.DMA((slabs,)),
            pltpu.SemaphoreType.DMA,
            pltpu.SemaphoreType.DMA((2 * slabs,)),
            pltpu.SemaphoreType.DMA((2 * slabs,)),
            pltpu.VMEM(tx.shape, BF16),
            pltpu.VMEM((half, LANES), jnp.int32),
            pltpu.VMEM((half, LANES), F32),
            pltpu.SemaphoreType.DMA((2,)),
        ],
        compiler_params=params(collective_id=0, has_side_effects=True),
    )(weights, wedge_sizes, wedge_scales, source_field[0], receiver_fields, model, tx, row_columns)

    returned = pl.pallas_call(
        functools.partial(shrink_back, shots, slabs, width),
        out_shape=jax.ShapeDtypeStruct((2 * slabs, slots, 2, pieces, planes, LANES), F32),
        grid=(slots,),
        in_specs=[
            whole_block(levels),
            whole_block(tz),
            whole_block(ty),
            pl.BlockSpec((None, pieces, depth * rows, LANES), lambda k: ((slots - 1 - k) // four, 0, 0, 0)),
        ],
        out_specs=anywhere,
        scratch_shapes=[
            pltpu.VMEM((2, depth, height), F32),
            pltpu.VMEM((slots, 2, pieces, depth, LANES), F32),
            pltpu.SemaphoreType.DMA((shots, slabs)),
            pltpu.SemaphoreType.DMA((2 * slabs,)),
            pltpu.SemaphoreType.DMA,
        ],
        compiler_params=params(collective_id=1, has_side_effects=True),
    )(levels, tz, ty, gathered)

    batch = math.gcd(planes, 2)
    terms = returned.reshape(2 * half * pieces * planes, LANES)
    return pl.pallas_call(
        functools.partial(inverse_x, planes, pieces),
        out_shape=jax.ShapeDtypeStruct((planes, height, width), F32),
        grid=(planes // batch,),
        in_specs=[whole_block(terms), whole_block(tx_back)],
        out_specs=pl.BlockSpec((batch, height, width), lambda z: (z, 0, 0)),
        compiler_params=params(),
    )(terms, tx_back)


def solution(mesh):
    placed = (
        P("shot", "slab", None, None),
        P("shot", "slab", None, None),
        P("shot"),
        P(("slab", "shot"), None, None),
        P(),
        P(),
    )
    return jax.shard_map(
        on_device,
        mesh=mesh,
        in_specs=placed,
        out_specs=P(("slab", "shot"), None, None),
        check_vma=False,
    )
```
